128 devices in a mesh: row: 8 (over z, core), col: 16 (over x, y).
Axes of the slice: x: 4, y: 4, z: 4, core: 2. Of those that a mesh axis runs over, the one named last changes fastest.
Arguments:
- nodes: bfloat16 [65536, 512], P(('row', 'col')), may hold values from -6 to 6
- cotangent: bfloat16 [65536, 512], P(('row', 'col')), may hold values from -6 to 6
- edge_source: int32 [262144], P(('row', 'col')), may hold values from 0 to 639
- edge_target: int32 [262144], P(('row', 'col')), may hold values from 0 to 511
- halo_lists: int32 [128, 4, 32], P(('row', 'col')), may hold values from 0 to 511
- pool_owner: int32 [65536], P(('row', 'col')), may hold values from 0 to 127, as said below
- pool_table: int32 [128, 1024], P(('row', 'col')), may hold values from -1 to 127, as said below
- source_weight: bfloat16 [512, 512], replicated, may hold values from -0.25 to 0.25
- target_weight: bfloat16 [512, 512], replicated, may hold values from -0.25 to 0.25
- edge_weight: bfloat16 [512, 512], replicated, may hold values from -0.25 to 0.25
- inner_weight: bfloat16 [1024, 512], replicated, may hold values from -0.1875 to 0.1875
- outer_weight: bfloat16 [512, 512], replicated, may hold values from -0.25 to 0.25
- coarse_weight: bfloat16 [512, 512], replicated, may hold values from -0.5 to 0.5
Outputs:
- updated: bfloat16 [65536, 512], P(('row', 'col'))
- node_gradient: float32 [65536, 512], P(('row', 'col'))
- source_gradient: float32 [512, 512], replicated
- target_gradient: float32 [512, 512], replicated
- edge_gradient: float32 [512, 512], replicated
- inner_gradient: float32 [1024, 512], replicated
- outer_gradient: float32 [512, 512], replicated
- coarse_gradient: float32 [512, 512], replicated
The draws below stay inside these ranges and needn't reach their ends.
Inputs may be any that keep to these rules, and one draw needn't show every extreme that they name: `edge_source`: rows below 512 are the partition's own nodes; row 512 + k * 32 + j is row j of halo block k. `pool_owner`: at most 8 nodes of one partition name the same owner; one owner is named by exactly 8 nodes of every partition. `pool_table`: entry [o, q * 8 + k] is the coarse row of owner o for the node of rank k among the nodes of partition q that name o, and -1 where q names o fewer than k + 1 times.
All inputs are finite; a program needn't handle non-finite values.
Results may differ from the reference program's by a relative error of at most 0.014.
Values may be sent and summed in bfloat16 or wider, within the bound.
No kernel may reach another device: no remote copies, remote signals or barrier semaphores. Data moves between devices by JAX's collectives and lax.ppermute only.
A program may use at most 128 MiB of HBM per device.

```python
import math
import jax
import jax.numpy as jnp
from jax import lax

W = 512
NODE_DEV = 512
EDGE_DEV = 2048
HALO = 32
COARSE_DEV = 128
CAP = 8
NODES = 65536
EDGES = 262144
N_ROW = 8
N_COL = 16
DEVICES = 128


def pooling_plan(key):
    busy_key = jax.random.fold_in(key, 11)
    score_key = jax.random.fold_in(key, 12)
    order_key = jax.random.fold_in(key, 13)
    row_key = jax.random.fold_in(key, 14)
    slots = DEVICES * CAP
    busy = jax.random.randint(busy_key, (), 0, DEVICES)
    places = jnp.arange(slots, dtype=jnp.int32)
    scores = jax.random.randint(score_key, (DEVICES, slots), 0, 32768) * slots + places[None, :]
    bucket = places // CAP
    scores = jnp.where((bucket == busy)[None, :], 2 ** 30 + places[None, :], scores)
    chosen = lax.top_k(scores, NODE_DEV)[1]
    chosen_owner = (chosen // CAP).astype(jnp.int32)
    counts = jnp.sum((chosen_owner[:, :, None] == jnp.arange(DEVICES, dtype=jnp.int32)[None, None, :]).astype(jnp.int32), axis=1)
    shuffle = jax.random.randint(order_key, (DEVICES, NODE_DEV), 0, 65536) * NODE_DEV + jnp.arange(NODE_DEV, dtype=jnp.int32)[None, :]
    order = jnp.argsort(shuffle, axis=1)
    owner = jnp.take_along_axis(chosen_owner, order, axis=1)
    live = jnp.arange(CAP, dtype=jnp.int32)[None, None, :] < counts[:, :, None]
    rows = jax.random.randint(row_key, (DEVICES, DEVICES, CAP), 0, COARSE_DEV)
    table = jnp.where(jnp.transpose(live, (1, 0, 2)), rows, -1).reshape(DEVICES, slots)
    return (owner.reshape(DEVICES * NODE_DEV).astype(jnp.int32), table.astype(jnp.int32))


def draw_pool_owner(key, part):
    return pooling_plan(key)[0]


def draw_pool_table(key, part):
    return pooling_plan(key)[1]


def set_ends(values, own_key, smallest, high):
    longest = values.shape.index(max(values.shape))
    spots = []
    for shift in (0, 1):
        where = [jax.random.randint(jax.random.fold_in(own_key, axis), (), 0, length) for axis, length in enumerate(values.shape)]
        where[longest] = (where[longest] + shift) % values.shape[longest]
        spots.append(tuple(where))
    return values.at[spots[0]].set(smallest).at[spots[1]].set(high)


def block_levels(key, shape, split, least, high):
    factor_of, own = 1.0, jax.random.fold_in(key, 6)
    for axis_at, parts in split:
        heights = jnp.exp(jax.random.uniform(jax.random.fold_in(own, axis_at), (parts,), jnp.float32, least / len(split), high / len(split)))
        factor_of = factor_of * jnp.repeat(heights, shape[axis_at] // parts).reshape([-1 if axis == axis_at else 1 for axis in range(len(shape))])
    return factor_of


def centred(key, extent, deviation, bound, cuts=(), held_as=jnp.bfloat16):
    drawn = jax.random.normal(key, extent, jnp.float32) * deviation
    if len(cuts) > 0:
        drawn = block_levels(key, extent, cuts, -0.22, 0.18) * drawn
    return jnp.clip(drawn, min=-bound, max=bound).astype(held_as)


def setup_inputs(seed: int = 0) -> dict:
    key_of = jax.random.split(jax.random.key(seed), 14)
    return {
        "nodes": centred(key_of[0], (NODES, W), 1.0, 6.0, ((0, 128),)),
        "cotangent": centred(key_of[1], (NODES, W), 1.0, 6.0, ((0, 128),)),
        "edge_source": set_ends(jax.random.randint(key_of[2], (EDGES,), 0, NODE_DEV + 4 * HALO), jax.random.fold_in(key_of[2], 1), 0, (NODE_DEV + 4 * HALO) - 1).astype(jnp.int32),
        "edge_target": set_ends(jax.random.randint(key_of[3], (EDGES,), 0, NODE_DEV), jax.random.fold_in(key_of[3], 1), 0, NODE_DEV - 1).astype(jnp.int32),
        "halo_lists": set_ends(jax.random.randint(key_of[4], (DEVICES, 4, HALO), 0, NODE_DEV), jax.random.fold_in(key_of[4], 1), 0, NODE_DEV - 1).astype(jnp.int32),
        "pool_owner": draw_pool_owner(jax.random.fold_in(key_of[13], 71), 0),
        "pool_table": draw_pool_table(jax.random.fold_in(key_of[13], 71), 0),
        "source_weight": centred(key_of[7], (W, W), W ** -0.5, 0.25),
        "target_weight": centred(key_of[8], (W, W), W ** -0.5, 0.25),
        "edge_weight": centred(key_of[9], (W, W), W ** -0.5, 0.25),
        "inner_weight": centred(key_of[10], (2 * W, W), (2 * W) ** -0.5, 0.1875),
        "outer_weight": centred(key_of[11], (W, W), W ** -0.5, 0.25),
        "coarse_weight": centred(key_of[12], (W, W), (W // 4) ** -0.5, 0.5),
    }


def product(first, second):
    return jnp.dot(first, second, preferred_element_type=jnp.float32)

def left_product(first, second):
    return lax.dot_general(first, second, (((0,), (0,)), ((), ())), preferred_element_type=jnp.float32)

def right_product(first, second):
    return lax.dot_general(first, second, (((1,), (1,)), ((), ())), preferred_element_type=jnp.float32)

def silu_slope(value):
    sigma = jax.nn.sigmoid(value)
    return sigma * (1.0 + value * (1.0 - sigma))

def shift_grid(blocks, axis, offset):
    length = blocks.shape[axis]
    rolled = jnp.roll(blocks, offset, axis=axis)
    anchor = jnp.arange(length) - offset
    keep = (anchor >= 0) & (anchor < length)
    shape = [1] * blocks.ndim
    shape[axis] = length
    return jnp.where(keep.reshape(shape), rolled, jnp.zeros_like(rolled))

def pick_rows(rows, lists):
    return jnp.take(rows, lists.reshape(-1), axis=0)

def add_returns(grads, lists, values):
    return grads.at[lists.reshape(-1)].add(values.astype(jnp.float32))

def local_forward(nodes_part, halo_part, source_part, target_part, weights):
    source_weight, target_weight, edge_weight, inner_weight, outer_weight = weights
    extended = jnp.concatenate([nodes_part, halo_part], axis=0)
    source_side = product(extended, source_weight)
    target_side = product(nodes_part, target_weight)
    edge_linear = jnp.take(source_side, source_part, axis=0) + jnp.take(target_side, target_part, axis=0)
    edge_hidden = jax.nn.silu(edge_linear).astype(jnp.bfloat16)
    message_linear = product(edge_hidden, edge_weight)
    aggregate = jax.ops.segment_sum(jax.nn.silu(message_linear), target_part, NODE_DEV).astype(jnp.bfloat16)
    joined = jnp.concatenate([nodes_part, aggregate], axis=1)
    node_linear = product(joined, inner_weight)
    node_hidden = jax.nn.silu(node_linear).astype(jnp.bfloat16)
    refined = (nodes_part.astype(jnp.float32) + product(node_hidden, outer_weight)).astype(jnp.bfloat16)
    return (extended, edge_linear, edge_hidden, message_linear, joined, node_linear, node_hidden, refined)

def reference(nodes, cotangent, edge_source, edge_target, halo_lists, pool_owner, pool_table, source_weight, target_weight, edge_weight, inner_weight, outer_weight, coarse_weight):
    weights = (source_weight, target_weight, edge_weight, inner_weight, outer_weight)
    node_parts = nodes.reshape(DEVICES, NODE_DEV, W)
    sent = jax.vmap(pick_rows)(node_parts, halo_lists).reshape(N_ROW, N_COL, 4, HALO, W)
    blocks = [shift_grid(sent[:, :, 0], 0, 1), shift_grid(sent[:, :, 1], 0, -1), shift_grid(sent[:, :, 2], 1, 1), shift_grid(sent[:, :, 3], 1, -1)]
    halo_parts = jnp.stack(blocks, axis=2).reshape(DEVICES, 4 * HALO, W)
    source_parts = edge_source.reshape(DEVICES, EDGE_DEV)
    target_parts = edge_target.reshape(DEVICES, EDGE_DEV)

    def forward_part(inputs):
        return local_forward(inputs[0], inputs[1], inputs[2], inputs[3], weights)[-1]
    refined = lax.map(forward_part, (node_parts, halo_parts, source_parts, target_parts)).reshape(NODES, W)
    owners = pool_owner.reshape(DEVICES, NODE_DEV)
    owner_hot = (owners[:, :, None] == jnp.arange(DEVICES, dtype=jnp.int32)[None, None, :]).astype(jnp.int32)
    rank = lax.optimization_barrier(jnp.sum((jnp.cumsum(owner_hot, axis=1) - 1) * owner_hot, axis=2)).astype(jnp.int32)
    column = jnp.arange(DEVICES, dtype=jnp.int32)[:, None] * CAP + rank
    parent = (owners * COARSE_DEV + pool_table[owners, column]).reshape(NODES).astype(jnp.int32)
    coarse_total = DEVICES * COARSE_DEV
    count = jnp.maximum(jax.ops.segment_sum(jnp.ones((NODES,), jnp.float32), parent, coarse_total), 1.0)[:, None]
    coarse = (jax.ops.segment_sum(refined.astype(jnp.float32), parent, coarse_total) / count).astype(jnp.bfloat16)
    coarse_linear = product(coarse, coarse_weight)
    coarse_update = jax.nn.silu(coarse_linear).astype(jnp.bfloat16)
    updated = (refined.astype(jnp.float32) + jnp.take(coarse_update, parent, axis=0).astype(jnp.float32)).astype(jnp.bfloat16)
    grad_coarse = (jax.ops.segment_sum(cotangent.astype(jnp.float32), parent, coarse_total) * silu_slope(coarse_linear)).astype(jnp.bfloat16)
    coarse_gradient = left_product(coarse, grad_coarse)
    coarse_share = (right_product(grad_coarse, coarse_weight) / count).astype(jnp.bfloat16)
    grad_refined = cotangent.astype(jnp.float32) + jnp.take(coarse_share, parent, axis=0).astype(jnp.float32)

    def backward_part(totals, inputs):
        nodes_part, halo_part, source_part, target_part, refined_grad = inputs
        extended, edge_linear, edge_hidden, message_linear, joined, node_linear, node_hidden, unused_rows = local_forward(nodes_part, halo_part, source_part, target_part, weights)
        refined_low = refined_grad.astype(jnp.bfloat16)
        outer_part = left_product(node_hidden, refined_low)
        grad_hidden = (right_product(refined_low, outer_weight) * silu_slope(node_linear)).astype(jnp.bfloat16)
        inner_part = left_product(joined, grad_hidden)
        grad_joined = right_product(grad_hidden, inner_weight)
        grad_aggregate = grad_joined[:, W:].astype(jnp.bfloat16)
        grad_message = (jnp.take(grad_aggregate, target_part, axis=0) * silu_slope(message_linear)).astype(jnp.bfloat16)
        edge_part = left_product(edge_hidden, grad_message)
        grad_edges = right_product(grad_message, edge_weight) * silu_slope(edge_linear)
        grad_sources = jax.ops.segment_sum(grad_edges, source_part, NODE_DEV + 4 * HALO).astype(jnp.bfloat16)
        grad_targets = jax.ops.segment_sum(grad_edges, target_part, NODE_DEV).astype(jnp.bfloat16)
        source_part_grad = left_product(extended, grad_sources)
        target_part_grad = left_product(nodes_part, grad_targets)
        grad_extended = right_product(grad_sources, source_weight)
        local_grad = refined_grad + grad_joined[:, :W] + right_product(grad_targets, target_weight) + grad_extended[:NODE_DEV]
        halo_grad = grad_extended[NODE_DEV:].astype(jnp.bfloat16)
        totals = (totals[0] + source_part_grad, totals[1] + target_part_grad, totals[2] + edge_part, totals[3] + inner_part, totals[4] + outer_part)
        return (totals, (local_grad, halo_grad))
    square = jnp.zeros((W, W), jnp.float32)
    start = (square, square, square, jnp.zeros((2 * W, W), jnp.float32), square)
    totals, outputs = lax.scan(backward_part, start, (node_parts, halo_parts, source_parts, target_parts, grad_refined.reshape(DEVICES, NODE_DEV, W)))
    local_grads, halo_grads = outputs
    halo_grid = halo_grads.reshape(N_ROW, N_COL, 4, HALO, W)
    back = [shift_grid(halo_grid[:, :, 0], 0, -1), shift_grid(halo_grid[:, :, 1], 0, 1), shift_grid(halo_grid[:, :, 2], 1, -1), shift_grid(halo_grid[:, :, 3], 1, 1)]
    returned = jnp.stack(back, axis=2).reshape(DEVICES, 4 * HALO, W)
    node_gradient = jax.vmap(add_returns)(local_grads, halo_lists, returned).reshape(NODES, W)
    scale = 1.0 / math.sqrt(NODES)
    return (updated, node_gradient, totals[0] * scale, totals[1] * scale, totals[2] * scale, totals[3] * scale, totals[4] * scale, coarse_gradient * scale)
```

```python
import math

import jax
import jax.numpy as jnp
from jax import lax
from jax.experimental import pallas as pl
from jax.experimental.pallas import tpu as pltpu
from jax.sharding import PartitionSpec as P

BF = jnp.bfloat16
F32 = jnp.float32
F16 = jnp.float16
LANES = 128
CHUNK = 512
CAPACITY = 8
LOW = 2.0 ** -10
HIGH = 2.0 ** 15


def dot(first, second):
    return jnp.dot(first, second, preferred_element_type=F32)


def left_dot(first, second):
    return lax.dot_general(
        first, second, (((0,), (0,)), ((), ())), preferred_element_type=F32
    )


def right_dot(first, second):
    return lax.dot_general(
        first, second, (((1,), (1,)), ((), ())), preferred_element_type=F32
    )


def iota(shape, axis):
    return lax.broadcasted_iota(jnp.int32, shape, axis)


def column(row):
    square = (LANES, LANES)
    eye = iota(square, 0) == iota(square, 1)
    spread = jnp.broadcast_to(row.astype(F32), square)
    return jnp.sum(jnp.where(eye, spread, 0.0), axis=1, keepdims=True).astype(jnp.int32)


def hot(mask):
    return jnp.where(mask, 1.0, 0.0).astype(BF)


def wide_column(row):
    return jnp.concatenate(
        [column(row[:, k : k + LANES]) for k in range(0, row.shape[1], LANES)], axis=0
    )


def wide_row(ref):
    return jnp.concatenate([ref[k : k + 1, :] for k in range(ref.shape[0])], axis=1)


def gates(value):
    sigma = 0.5 * jnp.tanh(0.5 * value) + 0.5
    active = value * sigma
    return active, sigma + active * (1.0 - sigma)


def halo_kernel(nodes, lists, out):
    picks = hot(column(lists[...]) == iota((LANES, nodes.shape[0]), 1))
    out[...] = dot(picks, nodes[...]).astype(BF)


def prepare_kernel(owner, cotangent, nodes, source_weight, target_weight, slot_out, sent, own_source, target_side):
    rows = nodes.shape[0]
    owner_row = wide_row(owner)
    owner_column = wide_column(owner_row)
    square = (rows, rows)
    before = (owner_column == owner_row) & (iota(square, 0) < iota(square, 1))
    rank = jnp.sum(jnp.where(before, 1.0, 0.0), axis=0, keepdims=True).astype(jnp.int32)
    slot = owner_row * CAPACITY + rank
    slot_out[...] = slot
    place = hot(iota((sent.shape[0], rows), 0) == slot)
    sent[...] = dot(place, cotangent[...]).astype(BF)
    own_source[...] = dot(nodes[...], source_weight[...]).astype(BF)
    target_side[...] = dot(nodes[...], target_weight[...]).astype(BF)


def forward_kernel(
    halo_0, halo_1, halo_2, halo_3, own_source, target_side, nodes, edge_source, edge_target, slot,
    source_weight, edge_weight, inner_weight, outer_weight,
    edge_hidden, edge_slope, message_slope, aggregate, node_hidden, node_slope, refined, sent,
    sides, active, spread,
):
    rows, width = nodes.shape
    extended = rows + LANES
    edges = edge_hidden.shape[0]
    sides[:rows, :] = own_source[...]
    halo = jnp.concatenate([halo_0[...], halo_1[...], halo_2[...], halo_3[...]], axis=0)
    sides[rows:extended, :] = dot(halo, source_weight[...]).astype(BF)
    sides[extended:, :] = target_side[...]
    group = CHUNK // LANES

    def step(turn, carry):
        span = pl.ds(pl.multiple_of(turn * CHUNK, CHUNK), CHUNK)
        picks = []
        for k in range(group):
            at = turn * group + k
            senders = edge_source[pl.ds(at, 1), :]
            receivers = edge_target[pl.ds(at, 1), :]
            place = iota((LANES, extended + rows), 1)
            picks.append(hot((column(senders) == place) | (column(receivers) + extended == place)))
            lanes = pl.ds(pl.multiple_of(at * LANES, LANES), LANES)
            spread[:, lanes] = hot(iota((rows, LANES), 0) == receivers)
        hidden, slope = gates(dot(jnp.concatenate(picks, axis=0), sides[...]))
        hidden = hidden.astype(BF)
        edge_hidden[span, :] = hidden
        edge_slope[span, :] = slope.astype(BF)
        message, slope = gates(dot(hidden, edge_weight[...]))
        active[span, :] = message.astype(BF)
        message_slope[span, :] = slope.astype(BF)
        return carry

    lax.fori_loop(0, edges // CHUNK, step, 0)
    gathered = dot(spread[...], active[...]).astype(BF)
    aggregate[...] = gathered
    linear = dot(nodes[...], inner_weight[:width, :]) + dot(gathered, inner_weight[width:, :])
    hidden, slope = gates(linear)
    hidden = hidden.astype(BF)
    node_hidden[...] = hidden
    node_slope[...] = slope.astype(BF)
    result = (nodes[...].astype(F32) + dot(hidden, outer_weight[...])).astype(BF)
    refined[...] = result
    place = hot(iota((sent.shape[0], rows), 0) == slot[...])
    sent[...] = dot(place, result).astype(BF)


def members_kernel(arrived, table, members, totals, counts):
    coarse = members.shape[0]
    row = wide_row(table)
    inside = iota((coarse, row.shape[1]), 0) == row
    ones = jnp.where(inside, 1.0, 0.0)
    members[...] = ones.astype(BF)
    count = jnp.maximum(jnp.sum(ones, axis=1, keepdims=True), 1.0)
    counts[...] = jnp.broadcast_to(count, counts.shape)
    totals[...] = dot(ones.astype(BF), arrived[...])


def coarse_kernel(arrived, members, totals, counts, table, weight, share_out, update, coarse_out, grad_out):
    count = counts[:, :1]
    coarse = (dot(members[...], arrived[...]) / count).astype(BF)
    coarse_out[...] = coarse
    active, slope = gates(dot(coarse, weight[...]))
    update[...] = active.astype(BF)
    grad = (totals[...] * slope).astype(BF)
    grad_out[...] = grad
    share = (right_dot(grad, weight[...]) / count).astype(BF)
    picks = hot(wide_column(wide_row(table)) == iota((share_out.shape[0], coarse.shape[0]), 1))
    share_out[...] = dot(picks, share).astype(BF)


def coarse_rest_kernel(scale, update, coarse, grad, table, update_out, gradient):
    picks = hot(wide_column(wide_row(table)) == iota((update_out.shape[0], update.shape[0]), 1))
    update_out[...] = dot(picks, update[...]).astype(BF)
    gradient[...] = left_dot(coarse[...], grad[...]) * scale


def node_back_kernel(
    scale, returned, slot, cotangent, nodes, aggregate, node_hidden, node_slope, inner_weight, outer_weight,
    grad_aggregate, base, outer_gradient, inner_gradient,
):
    rows, width = nodes.shape
    picks = hot(wide_column(slot[...]) == iota((rows, returned.shape[0]), 1))
    grad = cotangent[...].astype(F32) + dot(picks, returned[...])
    low = grad.astype(BF)
    hidden = (right_dot(low, outer_weight[...]) * node_slope[...].astype(F32)).astype(BF)
    grad_aggregate[...] = right_dot(hidden, inner_weight[width:, :]).astype(BF)
    base[...] = grad + right_dot(hidden, inner_weight[:width, :])
    outer_gradient[...] = left_dot(node_hidden[...], low) * scale
    inner_gradient[:width, :] = left_dot(nodes[...], hidden) * scale
    inner_gradient[width:, :] = left_dot(aggregate[...], hidden) * scale


def edge_back_kernel(
    edge_source, edge_target, grad_aggregate, edge_slope, message_slope, edge_weight, source_weight,
    grad_message, grad_edges, grad_sources, back,
    spread,
):
    edges, width = edge_slope.shape
    rows = grad_aggregate.shape[0]
    extended = grad_sources.shape[0]
    group = CHUNK // LANES

    def step(turn, carry):
        span = pl.ds(pl.multiple_of(turn * CHUNK, CHUNK), CHUNK)
        picks = []
        for k in range(group):
            at = turn * group + k
            receivers = edge_target[pl.ds(at, 1), :]
            picks.append(hot(column(receivers) == iota((LANES, rows), 1)))
            lanes = pl.ds(pl.multiple_of(at * LANES, LANES), LANES)
            spread[:, lanes] = hot(iota((extended, LANES), 0) == edge_source[pl.ds(at, 1), :])
        taken = dot(jnp.concatenate(picks, axis=0), grad_aggregate[...])
        message = (taken * message_slope[span, :].astype(F32)).astype(BF)
        grad_message[span, :] = message
        grad = right_dot(message, edge_weight[...]) * edge_slope[span, :].astype(F32)
        grad_edges[span, :] = grad.astype(BF)
        return carry

    lax.fori_loop(0, edges // CHUNK, step, 0)
    sums = dot(spread[...], grad_edges[...]).astype(BF)
    grad_sources[...] = sums
    back[...] = right_dot(sums[rows:, :], source_weight[...]).astype(BF)


def weights_kernel(
    scale, edge_target, edge_hidden, grad_message, grad_edges, grad_sources, halo_0, halo_1, halo_2, halo_3,
    nodes, base, source_weight, target_weight,
    source_gradient, target_gradient, edge_gradient, partial,
    spread,
):
    rows, width = nodes.shape
    for k in range(edge_target.shape[0]):
        spread[:, k * LANES : (k + 1) * LANES] = hot(iota((rows, LANES), 0) == edge_target[k : k + 1, :])
    targets = dot(spread[...], grad_edges[...]).astype(BF)
    sources = grad_sources[...]
    halo = jnp.concatenate([halo_0[...], halo_1[...], halo_2[...], halo_3[...]], axis=0)
    edge_gradient[...] = left_dot(edge_hidden[...], grad_message[...]) * scale
    source_gradient[...] = (left_dot(nodes[...], sources[:rows, :]) + left_dot(halo, sources[rows:, :])) * scale
    target_gradient[...] = left_dot(nodes[...], targets) * scale
    partial[...] = base[...] + right_dot(targets, target_weight[...]) + right_dot(sources[:rows, :], source_weight[...])


def node_gradient_kernel(partial, lists, back_0, back_1, back_2, back_3, out):
    back = jnp.concatenate([back_0[...], back_1[...], back_2[...], back_3[...]], axis=0)
    places = hot(iota((partial.shape[0], LANES), 0) == lists[...])
    out[...] = partial[...] + dot(places, back)


def updated_kernel(refined, returned, slot, out):
    picks = hot(wide_column(slot[...]) == iota((refined.shape[0], returned.shape[0]), 1))
    out[...] = (refined[...].astype(F32) + dot(picks, returned[...])).astype(BF)


def call(kernel, outs, *args, scratch=(), **static):
    import functools

    body = functools.partial(kernel, *static.values()) if static else kernel
    return pl.pallas_call(
        body,
        out_shape=[jax.ShapeDtypeStruct(shape, dtype) for shape, dtype in outs],
        scratch_shapes=[pltpu.VMEM(shape, dtype) for shape, dtype in scratch],
        compiler_params=pltpu.CompilerParams(vmem_limit_bytes=60 * 2 ** 20),
        name=kernel.__name__,
    )(*args)


def passed_along(value, axis, steps):
    count = lax.axis_size(axis)
    initial, last = (max(0, -steps), min(count, count - steps))
    return lax.ppermute(value, axis, [(source, source + steps) for source in range(initial, last)])


def trade_halo(blocks, flip):
    moved = []
    for number, offset in enumerate((1, -1)):
        moved.append(passed_along(blocks[number], "row", offset * flip))
    for number, offset in enumerate((1, -1)):
        moved.append(passed_along(blocks[2 + number], "col", offset * flip))
    return moved


def trade_slots(buffer, devices):
    slots, width = buffer.shape
    shaped = buffer.reshape(devices, slots // devices, width)
    moved = lax.all_to_all(shaped, ("row", "col"), split_axis=0, concat_axis=0, tiled=True)
    return moved.reshape(slots, width)


def summed(parts):
    stacked = jnp.concatenate(parts, axis=0)
    narrow = lax.psum(stacked.astype(F16), ("row", "col")).astype(F32)
    sizes = []
    for part in range(stacked.shape[0] // 512):
        block = narrow[part * 512 : (part + 1) * 512]
        sizes.append(jnp.mean(block * block))
    sizes = jnp.stack(sizes)
    fits = jnp.all(sizes > LOW * LOW) & (jnp.max(jnp.abs(narrow)) < HIGH)
    return lax.cond(
        fits,
        lambda narrow, stacked: narrow,
        lambda narrow, stacked: lax.psum(stacked, ("row", "col")),
        narrow,
        stacked,
    )


def local(
    nodes,
    cotangent,
    edge_source,
    edge_target,
    halo_lists,
    pool_owner,
    pool_table,
    source_weight,
    target_weight,
    edge_weight,
    inner_weight,
    outer_weight,
    coarse_weight,
):
    devices = lax.axis_size("row") * lax.axis_size("col")
    rows, width = nodes.shape
    edges = edge_source.shape[0]
    halo_rows = halo_lists.shape[2]
    extended = rows + 4 * halo_rows
    slots = pool_table.shape[1]
    coarse_rows = rows // 4
    scale = 1.0 / math.sqrt(rows * devices)
    lists = halo_lists.reshape(1, 4 * halo_rows)
    owner = pool_owner.reshape(rows // LANES, LANES)
    table = pool_table.reshape(slots // LANES, LANES)
    senders = edge_source.reshape(edges // LANES, LANES)
    receivers = edge_target.reshape(edges // LANES, LANES)
    node_block, edge_block = (rows, width), (edges, width)
    square = ((width, width), F32)

    (halo_sent,) = call(halo_kernel, [((4 * halo_rows, width), BF)], nodes, lists)
    sent_blocks = [halo_sent[k * halo_rows : (k + 1) * halo_rows] for k in range(4)]
    halo = trade_halo(sent_blocks, 1)
    slot, cot_sent, own_source, target_side = call(
        prepare_kernel,
        [((1, rows), jnp.int32), ((slots, width), BF), (node_block, BF), (node_block, BF)],
        owner, cotangent, nodes, source_weight, target_weight,
    )
    cot_arrived = trade_slots(cot_sent, devices)
    edge_hidden, edge_slope, message_slope, aggregate, node_hidden, node_slope, refined, sent = call(
        forward_kernel,
        [(edge_block, BF)] * 3 + [(node_block, BF)] * 4 + [((slots, width), BF)],
        *halo, own_source, target_side, nodes, senders, receivers, slot,
        source_weight, edge_weight, inner_weight, outer_weight,
        scratch=[((extended + rows, width), BF), (edge_block, BF), ((rows, edges), BF)],
    )
    arrived = trade_slots(sent, devices)
    members, totals, counts = call(
        members_kernel,
        [((coarse_rows, slots), BF), ((coarse_rows, width), F32), ((coarse_rows, LANES), F32)],
        cot_arrived, table,
    )
    share_sent, update, coarse, grad_coarse = call(
        coarse_kernel,
        [((slots, width), BF)] + [((coarse_rows, width), BF)] * 3,
        arrived, members, totals, counts, table, coarse_weight,
    )
    share_returned = trade_slots(share_sent, devices)
    update_sent, coarse_gradient = call(
        coarse_rest_kernel, [((slots, width), BF), square], update, coarse, grad_coarse, table, scale=scale
    )
    update_sent, share_returned = lax.optimization_barrier((update_sent, share_returned))
    update_returned = trade_slots(update_sent, devices)
    grad_aggregate, base, outer_gradient, inner_gradient = call(
        node_back_kernel,
        [(node_block, BF), (node_block, F32), square, ((2 * width, width), F32)],
        share_returned, slot, cotangent, nodes, aggregate, node_hidden, node_slope, inner_weight, outer_weight,
        scale=scale,
    )
    grad_message, grad_edges, grad_sources, back = call(
        edge_back_kernel,
        [(edge_block, BF), (edge_block, BF), ((extended, width), BF), ((4 * halo_rows, width), BF)],
        senders, receivers, grad_aggregate, edge_slope, message_slope, edge_weight, source_weight,
        scratch=[((extended, edges), BF)],
    )
    returned = trade_halo([back[k * halo_rows : (k + 1) * halo_rows] for k in range(4)], -1)
    source_gradient, target_gradient, edge_gradient, partial = call(
        weights_kernel,
        [square, square, square, (node_block, F32)],
        receivers, edge_hidden, grad_message, grad_edges, grad_sources, *halo,
        nodes, base, source_weight, target_weight,
        scratch=[((rows, edges), BF)],
        scale=scale,
    )
    (node_gradient,) = call(node_gradient_kernel, [(node_block, F32)], partial, lists, *returned)
    parts = [source_gradient, target_gradient, edge_gradient, inner_gradient, outer_gradient, coarse_gradient]
    sums = summed(parts)
    (updated,) = call(updated_kernel, [(node_block, BF)], refined, update_returned, slot)
    results, at = [], 0
    for part in parts:
        results.append(sums[at : at + part.shape[0]])
        at += part.shape[0]
    return (updated, node_gradient, *results)


def solution(mesh):
    in_specs = (
        P(("row", "col"), None),
        P(("row", "col"), None),
        P(("row", "col")),
        P(("row", "col")),
        P(("row", "col"), None, None),
        P(("row", "col")),
        P(("row", "col"), None),
        P(),
        P(),
        P(),
        P(),
        P(),
        P(),
    )
    out_specs = (P(("row", "col"), None), P(("row", "col"), None), P(), P(), P(), P(), P(), P())
    return jax.shard_map(local, mesh=mesh, in_specs=in_specs, out_specs=out_specs, check_vma=False)
```

```python
import functools
import math

import jax
import jax.numpy as jnp
from jax import lax
from jax.experimental import pallas as pl
from jax.experimental.pallas import tpu as pltpu
from jax.sharding import Mesh
from jax.sharding import PartitionSpec as P

BF = jnp.bfloat16
F32 = jnp.float32
LANES = 128
CHUNK = 512
CAPACITY = 8
ROW = ("z", "core")
COL = ("x", "y")
CHIPS = ("z", "x", "y")
ALL = ROW + COL


def dot(first, second):
    return jnp.dot(first, second, preferred_element_type=F32)


def left_dot(first, second):
    return lax.dot_general(
        first, second, (((0,), (0,)), ((), ())), preferred_element_type=F32
    )


def right_dot(first, second):
    return lax.dot_general(
        first, second, (((1,), (1,)), ((), ())), preferred_element_type=F32
    )


def iota(shape, axis):
    return lax.broadcasted_iota(jnp.int32, shape, axis)


def column(row):
    square = (LANES, LANES)
    eye = iota(square, 0) == iota(square, 1)
    spread = jnp.broadcast_to(row.astype(F32), square)
    return jnp.sum(jnp.where(eye, spread, 0.0), axis=1, keepdims=True).astype(jnp.int32)


def hot(mask):
    return jnp.where(mask, 1.0, 0.0).astype(BF)


def wide_column(row):
    return jnp.concatenate(
        [column(row[:, k : k + LANES]) for k in range(0, row.shape[1], LANES)], axis=0
    )


def wide_row(ref):
    return jnp.concatenate([ref[k : k + 1, :] for k in range(ref.shape[0])], axis=1)


def gates(value):
    sigma = 0.5 * jnp.tanh(0.5 * value) + 0.5
    active = value * sigma
    return active, sigma + active * (1.0 - sigma)


def halo_kernel(nodes, lists, out):
    picks = hot(column(lists[...]) == iota((LANES, nodes.shape[0]), 1))
    out[...] = dot(picks, nodes[...]).astype(BF)


def prepare_kernel(owner, cotangent, nodes, source_weight, target_weight, slot_out, sent, own_source, target_side):
    rows = nodes.shape[0]
    owner_row = wide_row(owner)
    owner_column = wide_column(owner_row)
    square = (rows, rows)
    before = (owner_column == owner_row) & (iota(square, 0) < iota(square, 1))
    rank = jnp.sum(jnp.where(before, 1.0, 0.0), axis=0, keepdims=True).astype(jnp.int32)
    slot = owner_row * CAPACITY + rank
    slot_out[...] = slot
    place = hot(iota((sent.shape[0], rows), 0) == slot)
    sent[...] = dot(place, cotangent[...]).astype(BF)
    own_source[...] = dot(nodes[...], source_weight[...]).astype(BF)
    target_side[...] = dot(nodes[...], target_weight[...]).astype(BF)


def forward_kernel(
    halo_0, halo_1, halo_2, halo_3, own_source, target_side, nodes, edge_source, edge_target, slot,
    source_weight, edge_weight, inner_weight, outer_weight,
    edge_hidden, edge_slope, message_slope, aggregate, node_hidden, node_slope, refined, sent,
    sides, active, spread,
):
    rows, width = nodes.shape
    extended = rows + LANES
    edges = edge_hidden.shape[0]
    sides[:rows, :] = own_source[...]
    halo = jnp.concatenate([halo_0[...], halo_1[...], halo_2[...], halo_3[...]], axis=0)
    sides[rows:extended, :] = dot(halo, source_weight[...]).astype(BF)
    sides[extended:, :] = target_side[...]
    group = CHUNK // LANES

    def step(turn, carry):
        span = pl.ds(pl.multiple_of(turn * CHUNK, CHUNK), CHUNK)
        picks = []
        for k in range(group):
            at = turn * group + k
            senders = edge_source[pl.ds(at, 1), :]
            receivers = edge_target[pl.ds(at, 1), :]
            place = iota((LANES, extended + rows), 1)
            picks.append(hot((column(senders) == place) | (column(receivers) + extended == place)))
            lanes = pl.ds(pl.multiple_of(at * LANES, LANES), LANES)
            spread[:, lanes] = hot(iota((rows, LANES), 0) == receivers)
        hidden, slope = gates(dot(jnp.concatenate(picks, axis=0), sides[...]))
        hidden = hidden.astype(BF)
        edge_hidden[span, :] = hidden
        edge_slope[span, :] = slope.astype(BF)
        message, slope = gates(dot(hidden, edge_weight[...]))
        active[span, :] = message.astype(BF)
        message_slope[span, :] = slope.astype(BF)
        return carry

    lax.fori_loop(0, edges // CHUNK, step, 0)
    gathered = dot(spread[...], active[...]).astype(BF)
    aggregate[...] = gathered
    linear = dot(nodes[...], inner_weight[:width, :]) + dot(gathered, inner_weight[width:, :])
    hidden, slope = gates(linear)
    hidden = hidden.astype(BF)
    node_hidden[...] = hidden
    node_slope[...] = slope.astype(BF)
    result = (nodes[...].astype(F32) + dot(hidden, outer_weight[...])).astype(BF)
    refined[...] = result
    place = hot(iota((sent.shape[0], rows), 0) == slot[...])
    sent[...] = dot(place, result).astype(BF)


def members_kernel(arrived, table, members, totals, counts):
    coarse = members.shape[0]
    row = wide_row(table)
    inside = iota((coarse, row.shape[1]), 0) == row
    ones = jnp.where(inside, 1.0, 0.0)
    members[...] = ones.astype(BF)
    count = jnp.maximum(jnp.sum(ones, axis=1, keepdims=True), 1.0)
    counts[...] = jnp.broadcast_to(count, counts.shape)
    totals[...] = dot(ones.astype(BF), arrived[...])


def coarse_kernel(arrived, members, totals, counts, table, weight, share_out, update, coarse_out, grad_out):
    count = counts[:, :1]
    coarse = (dot(members[...], arrived[...]) / count).astype(BF)
    coarse_out[...] = coarse
    active, slope = gates(dot(coarse, weight[...]))
    update[...] = active.astype(BF)
    grad = (totals[...] * slope).astype(BF)
    grad_out[...] = grad
    share = (right_dot(grad, weight[...]) / count).astype(BF)
    picks = hot(wide_column(wide_row(table)) == iota((share_out.shape[0], coarse.shape[0]), 1))
    share_out[...] = dot(picks, share).astype(BF)


def coarse_rest_kernel(update, table, update_out):
    picks = hot(wide_column(wide_row(table)) == iota((update_out.shape[0], update.shape[0]), 1))
    update_out[...] = dot(picks, update[...]).astype(BF)


def half_of(ref, half):
    columns = ref.shape[1] // 2
    return ref[:, pl.ds(pl.multiple_of(half * columns, columns), columns)]


def pack(out, at, value):
    rows, width = value.shape
    for k in range(width // LANES):
        out[at * width // LANES + k * rows : at * width // LANES + (k + 1) * rows, :] = value[
            :, k * LANES : (k + 1) * LANES
        ].astype(BF)


def halves(scale, core, keep, give, pairs):
    at = 0
    for first, second in pairs:
        for out, half in ((keep, core[0]), (give, 1 - core[0])):
            pack(out, at, left_dot(half_of(first, half), second) * scale)
        at += first.shape[1] // 2


def node_back_kernel(
    scale, core, returned, slot, cotangent, nodes, aggregate, node_hidden, node_slope, coarse, grad_coarse,
    inner_weight, outer_weight,
    grad_aggregate, base, keep, give,
):
    rows, width = nodes.shape
    picks = hot(wide_column(slot[...]) == iota((rows, returned.shape[0]), 1))
    grad = cotangent[...].astype(F32) + dot(picks, returned[...])
    low = grad.astype(BF)
    hidden = (right_dot(low, outer_weight[...]) * node_slope[...].astype(F32)).astype(BF)
    grad_aggregate[...] = right_dot(hidden, inner_weight[width:, :]).astype(BF)
    base[...] = grad + right_dot(hidden, inner_weight[:width, :])
    pairs = ((node_hidden, low), (nodes, hidden), (aggregate, hidden), (coarse, grad_coarse[...]))
    halves(scale, core, keep, give, pairs)


def edge_back_kernel(
    edge_source, edge_target, grad_aggregate, edge_slope, message_slope, edge_weight, source_weight,
    grad_message, grad_edges, grad_sources, back,
    spread,
):
    edges, width = edge_slope.shape
    rows = grad_aggregate.shape[0]
    extended = grad_sources.shape[0]
    group = CHUNK // LANES

    def step(turn, carry):
        span = pl.ds(pl.multiple_of(turn * CHUNK, CHUNK), CHUNK)
        picks = []
        for k in range(group):
            at = turn * group + k
            receivers = edge_target[pl.ds(at, 1), :]
            picks.append(hot(column(receivers) == iota((LANES, rows), 1)))
            lanes = pl.ds(pl.multiple_of(at * LANES, LANES), LANES)
            spread[:, lanes] = hot(iota((extended, LANES), 0) == edge_source[pl.ds(at, 1), :])
        taken = dot(jnp.concatenate(picks, axis=0), grad_aggregate[...])
        message = (taken * message_slope[span, :].astype(F32)).astype(BF)
        grad_message[span, :] = message
        grad = right_dot(message, edge_weight[...]) * edge_slope[span, :].astype(F32)
        grad_edges[span, :] = grad.astype(BF)
        return carry

    lax.fori_loop(0, edges // CHUNK, step, 0)
    sums = dot(spread[...], grad_edges[...]).astype(BF)
    grad_sources[...] = sums
    back[...] = right_dot(sums[rows:, :], source_weight[...]).astype(BF)


def weights_kernel(
    scale, core, edge_target, edge_hidden, grad_message, grad_edges, grad_sources, halo_0, halo_1, halo_2, halo_3,
    nodes, base, source_weight, target_weight,
    keep, give, partial,
    spread, extended,
):
    rows, width = nodes.shape
    for k in range(edge_target.shape[0]):
        spread[:, k * LANES : (k + 1) * LANES] = hot(iota((rows, LANES), 0) == edge_target[k : k + 1, :])
    targets = dot(spread[...], grad_edges[...]).astype(BF)
    sources = grad_sources[...]
    extended[:rows, :] = nodes[...]
    extended[rows:, :] = jnp.concatenate([halo_0[...], halo_1[...], halo_2[...], halo_3[...]], axis=0)
    pairs = ((edge_hidden, grad_message[...]), (extended, sources), (nodes, targets))
    halves(scale, core, keep, give, pairs)
    partial[...] = base[...] + right_dot(targets, target_weight[...]) + right_dot(sources[:rows, :], source_weight[...])


def node_gradient_kernel(partial, lists, back_0, back_1, back_2, back_3, out):
    back = jnp.concatenate([back_0[...], back_1[...], back_2[...], back_3[...]], axis=0)
    places = hot(iota((partial.shape[0], LANES), 0) == lists[...])
    out[...] = partial[...] + dot(places, back)


def updated_kernel(refined, returned, slot, out):
    picks = hot(wide_column(slot[...]) == iota((refined.shape[0], returned.shape[0]), 1))
    out[...] = (refined[...].astype(F32) + dot(picks, returned[...])).astype(BF)


def pair_kernel(first, second, out):
    out[...] = (first[...].astype(F32) + second[...].astype(F32)).astype(BF)


def total_kernel(arrived, out):
    out[...] = jnp.sum(arrived[...].astype(F32), axis=0).astype(BF)


def spread_kernel(early, arrived, out):
    late = jnp.sum(arrived[...].astype(F32), axis=0).astype(BF)
    rows = early.shape[0]
    peers = out.shape[0]
    out[:, :rows, :] = jnp.broadcast_to(early[...][None], (peers, rows, LANES))
    out[:, rows:, :] = jnp.broadcast_to(late[None], (peers,) + late.shape)


def results_kernel(early, core, mine, other, source, target, edge, inner, outer, coarse):
    width = outer.shape[0]
    half = width // 2
    blocks = width // LANES
    for gathered, which in ((mine, core[0]), (other, 1 - core[0])):
        peers, rows, lanes = gathered.shape
        first = gathered[:, :early, :].astype(F32).reshape(peers * early, lanes)
        second = gathered[:, early:, :].astype(F32).reshape(peers * (rows - early), lanes)
        places = ((outer, 0, first), (inner, 0, first), (inner, width, first), (coarse, 0, first))
        places += ((edge, 0, second), (source, 0, second), (target, 0, second))
        for number, (out, base, values) in enumerate(places):
            at = (number if number < 4 else number - 4) * blocks * half
            span = pl.ds(pl.multiple_of(base + which * half, half), half)
            for k in range(blocks):
                out[span, k * LANES : (k + 1) * LANES] = values[at + k * half : at + (k + 1) * half, :]


def call(kernel, outs, *args, scratch=(), core=None, **static):
    body = functools.partial(kernel, *static.values())
    specs = [pl.BlockSpec(memory_space=pltpu.VMEM)] * len(args)
    if core is not None:
        args, specs = (core,) + args, [pl.BlockSpec(memory_space=pltpu.SMEM)] + specs
    return pl.pallas_call(
        body,
        in_specs=specs,
        out_shape=[jax.ShapeDtypeStruct(shape, dtype) for shape, dtype in outs],
        scratch_shapes=[pltpu.VMEM(shape, dtype) for shape, dtype in scratch],
        compiler_params=pltpu.CompilerParams(vmem_limit_bytes=60 * 2 ** 20),
        name=kernel.__name__,
    )(*args)


def passed_along(value, axis, steps):
    count = math.prod(lax.axis_size(name) for name in axis)
    initial, last = (max(0, -steps), min(count, count - steps))
    return lax.ppermute(value, axis, [(source, source + steps) for source in range(initial, last)])


def trade_halo(blocks, flip):
    moved = []
    for number, offset in enumerate((1, -1)):
        moved.append(passed_along(blocks[number], ROW, offset * flip))
    for number, offset in enumerate((1, -1)):
        moved.append(passed_along(blocks[2 + number], COL, offset * flip))
    return moved


def trade_slots(buffer, devices):
    slots, width = buffer.shape
    shaped = buffer.reshape(devices, slots // devices, width)
    moved = lax.all_to_all(shaped, ALL, split_axis=0, concat_axis=0, tiled=True)
    return moved.reshape(slots, width)


def across(value):
    return lax.ppermute(value, "core", [(0, 1), (1, 0)])


def trade_chips(value):
    return lax.all_to_all(value, CHIPS, split_axis=0, concat_axis=0, tiled=True)


def local(
    nodes,
    cotangent,
    edge_source,
    edge_target,
    halo_lists,
    pool_owner,
    pool_table,
    source_weight,
    target_weight,
    edge_weight,
    inner_weight,
    outer_weight,
    coarse_weight,
):
    chips = math.prod(lax.axis_size(name) for name in CHIPS)
    devices = 2 * chips
    core = lax.axis_index("core").reshape(1)
    rows, width = nodes.shape
    edges = edge_source.shape[0]
    halo_rows = halo_lists.shape[2]
    extended = rows + 4 * halo_rows
    slots = pool_table.shape[1]
    coarse_rows = rows // 4
    scale = 1.0 / math.sqrt(rows * devices)
    lists = halo_lists.reshape(1, 4 * halo_rows)
    owner = pool_owner.reshape(rows // LANES, LANES)
    table = pool_table.reshape(slots // LANES, LANES)
    senders = edge_source.reshape(edges // LANES, LANES)
    receivers = edge_target.reshape(edges // LANES, LANES)
    node_block, edge_block = (rows, width), (edges, width)
    square = ((width, width), F32)
    packed = width // 2 * width // LANES

    (halo_sent,) = call(halo_kernel, [((4 * halo_rows, width), BF)], nodes, lists)
    sent_blocks = [halo_sent[k * halo_rows : (k + 1) * halo_rows] for k in range(4)]
    halo = trade_halo(sent_blocks, 1)
    slot, cot_sent, own_source, target_side = call(
        prepare_kernel,
        [((1, rows), jnp.int32), ((slots, width), BF), (node_block, BF), (node_block, BF)],
        owner, cotangent, nodes, source_weight, target_weight,
    )
    cot_arrived = trade_slots(cot_sent, devices)
    edge_hidden, edge_slope, message_slope, aggregate, node_hidden, node_slope, refined, sent = call(
        forward_kernel,
        [(edge_block, BF)] * 3 + [(node_block, BF)] * 4 + [((slots, width), BF)],
        *halo, own_source, target_side, nodes, senders, receivers, slot,
        source_weight, edge_weight, inner_weight, outer_weight,
        scratch=[((extended + rows, width), BF), (edge_block, BF), ((rows, edges), BF)],
    )
    arrived = trade_slots(sent, devices)
    members, totals, counts = call(
        members_kernel,
        [((coarse_rows, slots), BF), ((coarse_rows, width), F32), ((coarse_rows, LANES), F32)],
        cot_arrived, table,
    )
    share_sent, update, coarse, grad_coarse = call(
        coarse_kernel,
        [((slots, width), BF)] + [((coarse_rows, width), BF)] * 3,
        arrived, members, totals, counts, table, coarse_weight,
    )
    share_returned = trade_slots(share_sent, devices)
    (update_sent,) = call(coarse_rest_kernel, [((slots, width), BF)], update, table)
    update_returned = trade_slots(update_sent, devices)
    grad_aggregate, base, keep, give = call(
        node_back_kernel,
        [(node_block, BF), (node_block, F32), ((4 * packed, LANES), BF), ((4 * packed, LANES), BF)],
        share_returned, slot, cotangent, nodes, aggregate, node_hidden, node_slope, coarse, grad_coarse,
        inner_weight, outer_weight,
        core=core, scale=scale,
    )
    taken = across(give)
    grad_message, grad_edges, grad_sources, back = call(
        edge_back_kernel,
        [(edge_block, BF), (edge_block, BF), ((extended, width), BF), ((4 * halo_rows, width), BF)],
        senders, receivers, grad_aggregate, edge_slope, message_slope, edge_weight, source_weight,
        scratch=[((extended, edges), BF)],
    )
    (early,) = call(pair_kernel, [((4 * packed, LANES), BF)], keep, taken)
    early_rows = 4 * packed // chips
    early = trade_chips(early.reshape(chips, early_rows, LANES))
    returned = trade_halo([back[k * halo_rows : (k + 1) * halo_rows] for k in range(4)], -1)
    keep, give, partial = call(
        weights_kernel,
        [((3 * packed, LANES), BF), ((3 * packed, LANES), BF), (node_block, F32)],
        receivers, edge_hidden, grad_message, grad_edges, grad_sources, *halo,
        nodes, base, source_weight, target_weight,
        scratch=[((rows, edges), BF), ((extended, width), BF)],
        core=core, scale=scale,
    )
    (late,) = call(pair_kernel, [((3 * packed, LANES), BF)], keep, across(give))
    late_rows = 3 * packed // chips
    late = trade_chips(late.reshape(chips, late_rows, LANES))
    (early,) = call(total_kernel, [((early_rows, LANES), BF)], early)
    (sent,) = call(spread_kernel, [((chips, early_rows + late_rows, LANES), BF)], early, late)
    mine = trade_chips(sent)
    (node_gradient,) = call(node_gradient_kernel, [(node_block, F32)], partial, lists, *returned)
    (updated,) = call(updated_kernel, [(node_block, BF)], refined, update_returned, slot)
    results = call(
        results_kernel,
        [square, square, square, ((2 * width, width), F32), square, square],
        mine, across(mine),
        core=core, early=early_rows,
    )
    return (updated, node_gradient, *results)


def solution(mesh):
    whole = mesh.devices.reshape(mesh.shape["row"] // 2, 2, -1, 4)
    mesh = Mesh(whole, ALL)
    in_specs = (
        P(ALL, None),
        P(ALL, None),
        P(ALL),
        P(ALL),
        P(ALL, None, None),
        P(ALL),
        P(ALL, None),
        P(),
        P(),
        P(),
        P(),
        P(),
        P(),
    )
    out_specs = (P(ALL, None), P(ALL, None), P(), P(), P(), P(), P(), P())
    return jax.shard_map(local, mesh=mesh, in_specs=in_specs, out_specs=out_specs, check_vma=False)
```

```python
import functools
import math

import jax
import jax.numpy as jnp
from jax import lax
from jax.experimental import pallas as pl
from jax.experimental.pallas import tpu as pltpu
from jax.sharding import Mesh
from jax.sharding import PartitionSpec as P


BF = jnp.bfloat16
F32 = jnp.float32
LANES = 128
CHUNK = 512
CAPACITY = 8
ROW = ("z", "core")
COL = ("x", "y")
CHIPS = ("z", "x", "y")
ALL = ROW + COL


def dot(first, second):
    return jnp.dot(first, second, preferred_element_type=F32)


def left_dot(first, second):
    return lax.dot_general(
        first, second, (((0,), (0,)), ((), ())), preferred_element_type=F32
    )


def right_dot(first, second):
    return lax.dot_general(
        first, second, (((1,), (1,)), ((), ())), preferred_element_type=F32
    )


def iota(shape, axis):
    return lax.broadcasted_iota(jnp.int32, shape, axis)


def column(row):
    square = (LANES, LANES)
    eye = iota(square, 0) == iota(square, 1)
    spread = jnp.broadcast_to(row.astype(F32), square)
    return jnp.sum(jnp.where(eye, spread, 0.0), axis=1, keepdims=True).astype(jnp.int32)


def hot(mask):
    return jnp.where(mask, 1.0, 0.0).astype(BF)


def wide_column(row):
    return jnp.concatenate(
        [column(row[:, k : k + LANES]) for k in range(0, row.shape[1], LANES)], axis=0
    )


def wide_row(ref):
    return jnp.concatenate([ref[k : k + 1, :] for k in range(ref.shape[0])], axis=1)


def gates(value):
    sigma = 0.5 * jnp.tanh(0.5 * value) + 0.5
    active = value * sigma
    return active, sigma + active * (1.0 - sigma)


def halo_kernel(nodes, lists, out):
    picks = hot(column(lists[...]) == iota((LANES, nodes.shape[0]), 1))
    out[...] = dot(picks, nodes[...]).astype(BF)


def prepare_kernel(owner, cotangent, nodes, source_weight, target_weight, slot_out, sent, own_source, target_side):
    rows = nodes.shape[0]
    owner_row = wide_row(owner)
    owner_column = wide_column(owner_row)
    square = (rows, rows)
    before = (owner_column == owner_row) & (iota(square, 0) < iota(square, 1))
    rank = jnp.sum(jnp.where(before, 1.0, 0.0), axis=0, keepdims=True).astype(jnp.int32)
    slot = owner_row * CAPACITY + rank
    slot_out[...] = slot
    place = hot(iota((sent.shape[0], rows), 0) == slot)
    sent[...] = dot(place, cotangent[...]).astype(BF)
    own_source[...] = dot(nodes[...], source_weight[...]).astype(BF)
    target_side[...] = dot(nodes[...], target_weight[...]).astype(BF)


def forward_kernel(
    halo_0, halo_1, halo_2, halo_3, own_source, target_side, nodes, edge_source, edge_target, slot,
    source_weight, edge_weight, inner_weight, outer_weight,
    edge_hidden, edge_slope, message_slope, aggregate, node_hidden, node_slope, refined, sent,
    sides, active, spread,
):
    rows, width = nodes.shape
    extended = rows + LANES
    edges = edge_hidden.shape[0]
    sides[:rows, :] = own_source[...]
    halo = jnp.concatenate([halo_0[...], halo_1[...], halo_2[...], halo_3[...]], axis=0)
    sides[rows:extended, :] = dot(halo, source_weight[...]).astype(BF)
    sides[extended:, :] = target_side[...]
    group = CHUNK // LANES

    def step(turn, carry):
        span = pl.ds(pl.multiple_of(turn * CHUNK, CHUNK), CHUNK)
        picks = []
        for k in range(group):
            at = turn * group + k
            senders = edge_source[pl.ds(at, 1), :]
            receivers = edge_target[pl.ds(at, 1), :]
            place = iota((LANES, extended + rows), 1)
            picks.append(hot((column(senders) == place) | (column(receivers) + extended == place)))
            lanes = pl.ds(pl.multiple_of(at * LANES, LANES), LANES)
            spread[:, lanes] = hot(iota((rows, LANES), 0) == receivers)
        hidden, slope = gates(dot(jnp.concatenate(picks, axis=0), sides[...]))
        hidden = hidden.astype(BF)
        edge_hidden[span, :] = hidden
        edge_slope[span, :] = slope.astype(BF)
        message, slope = gates(dot(hidden, edge_weight[...]))
        active[span, :] = message.astype(BF)
        message_slope[span, :] = slope.astype(BF)
        return carry

    lax.fori_loop(0, edges // CHUNK, step, 0)
    gathered = dot(spread[...], active[...]).astype(BF)
    aggregate[...] = gathered
    linear = dot(nodes[...], inner_weight[:width, :]) + dot(gathered, inner_weight[width:, :])
    hidden, slope = gates(linear)
    hidden = hidden.astype(BF)
    node_hidden[...] = hidden
    node_slope[...] = slope.astype(BF)
    result = (nodes[...].astype(F32) + dot(hidden, outer_weight[...])).astype(BF)
    refined[...] = result
    place = hot(iota((sent.shape[0], rows), 0) == slot[...])
    sent[...] = dot(place, result).astype(BF)


def members_kernel(arrived, table, members, totals, counts):
    coarse = members.shape[0]
    row = wide_row(table)
    inside = iota((coarse, row.shape[1]), 0) == row
    ones = jnp.where(inside, 1.0, 0.0)
    members[...] = ones.astype(BF)
    count = jnp.maximum(jnp.sum(ones, axis=1, keepdims=True), 1.0)
    counts[...] = jnp.broadcast_to(count, counts.shape)
    totals[...] = dot(ones.astype(BF), arrived[...])


def coarse_kernel(arrived, members, totals, counts, table, weight, out, coarse_out, grad_out):
    count = counts[:, :1]
    coarse = (dot(members[...], arrived[...]) / count).astype(BF)
    coarse_out[...] = coarse
    active, slope = gates(dot(coarse, weight[...]))
    grad = (totals[...] * slope).astype(BF)
    grad_out[...] = grad
    share = (right_dot(grad, weight[...]) / count).astype(BF)
    picks = hot(wide_column(wide_row(table)) == iota((out.shape[0], coarse.shape[0]), 1))
    out[...] = dot(picks, jnp.concatenate([share, active.astype(BF)], axis=1)).astype(BF)


def half_of(ref, half):
    columns = ref.shape[1] // 2
    return ref[:, pl.ds(pl.multiple_of(half * columns, columns), columns)]


def pack(out, at, value):
    rows, width = value.shape
    for k in range(width // LANES):
        out[at * width // LANES + k * rows : at * width // LANES + (k + 1) * rows, :] = value[
            :, k * LANES : (k + 1) * LANES
        ].astype(BF)


def halves(scale, core, keep, give, pairs):
    at = 0
    for first, second in pairs:
        for out, half in ((keep, core[0]), (give, 1 - core[0])):
            pack(out, at, left_dot(half_of(first, half), second) * scale)
        at += first.shape[1] // 2


def node_back_kernel(
    scale, core, returned, slot, cotangent, nodes, aggregate, node_hidden, node_slope, coarse, grad_coarse,
    inner_weight, outer_weight,
    grad_aggregate, base, keep, give,
):
    rows, width = nodes.shape
    picks = hot(wide_column(slot[...]) == iota((rows, returned.shape[0]), 1))
    grad = cotangent[...].astype(F32) + dot(picks, returned[:, :width])
    low = grad.astype(BF)
    hidden = (right_dot(low, outer_weight[...]) * node_slope[...].astype(F32)).astype(BF)
    grad_aggregate[...] = right_dot(hidden, inner_weight[width:, :]).astype(BF)
    base[...] = grad + right_dot(hidden, inner_weight[:width, :])
    pairs = ((node_hidden, low), (nodes, hidden), (aggregate, hidden), (coarse, grad_coarse[...]))
    halves(scale, core, keep, give, pairs)


def edge_back_kernel(
    edge_source, edge_target, grad_aggregate, edge_slope, message_slope, edge_weight, source_weight,
    grad_message, grad_edges, grad_sources, back,
    spread,
):
    edges, _ = edge_slope.shape
    rows = grad_aggregate.shape[0]
    extended = grad_sources.shape[0]
    group = CHUNK // LANES

    def step(turn, carry):
        span = pl.ds(pl.multiple_of(turn * CHUNK, CHUNK), CHUNK)
        picks = []
        for k in range(group):
            at = turn * group + k
            receivers = edge_target[pl.ds(at, 1), :]
            picks.append(hot(column(receivers) == iota((LANES, rows), 1)))
            lanes = pl.ds(pl.multiple_of(at * LANES, LANES), LANES)
            spread[:, lanes] = hot(iota((extended, LANES), 0) == edge_source[pl.ds(at, 1), :])
        taken = dot(jnp.concatenate(picks, axis=0), grad_aggregate[...])
        message = (taken * message_slope[span, :].astype(F32)).astype(BF)
        grad_message[span, :] = message
        grad = right_dot(message, edge_weight[...]) * edge_slope[span, :].astype(F32)
        grad_edges[span, :] = grad.astype(BF)
        return carry

    lax.fori_loop(0, edges // CHUNK, step, 0)
    sums = dot(spread[...], grad_edges[...]).astype(BF)
    grad_sources[...] = sums
    back[...] = right_dot(sums[rows:, :], source_weight[...]).astype(BF)


def weights_kernel(
    scale, core, edge_target, edge_hidden, grad_message, grad_edges, grad_sources, halo_0, halo_1, halo_2, halo_3,
    nodes, base, source_weight, target_weight,
    keep, give, partial,
    spread, extended,
):
    rows, _ = nodes.shape
    for k in range(edge_target.shape[0]):
        spread[:, k * LANES : (k + 1) * LANES] = hot(iota((rows, LANES), 0) == edge_target[k : k + 1, :])
    targets = dot(spread[...], grad_edges[...]).astype(BF)
    sources = grad_sources[...]
    extended[:rows, :] = nodes[...]
    extended[rows:, :] = jnp.concatenate([halo_0[...], halo_1[...], halo_2[...], halo_3[...]], axis=0)
    pairs = ((edge_hidden, grad_message[...]), (extended, sources), (nodes, targets))
    halves(scale, core, keep, give, pairs)
    partial[...] = base[...] + right_dot(targets, target_weight[...]) + right_dot(sources[:rows, :], source_weight[...])


def node_gradient_kernel(partial, lists, back_0, back_1, back_2, back_3, out):
    back = jnp.concatenate([back_0[...], back_1[...], back_2[...], back_3[...]], axis=0)
    places = hot(iota((partial.shape[0], LANES), 0) == lists[...])
    out[...] = partial[...] + dot(places, back)


def updated_kernel(refined, returned, slot, out):
    rows, width = refined.shape
    picks = hot(wide_column(slot[...]) == iota((rows, returned.shape[0]), 1))
    out[...] = (refined[...].astype(F32) + dot(picks, returned[:, width:])).astype(BF)


def results_kernel(early, core, mine, other, source, target, edge, inner, outer, coarse):
    width = outer.shape[0]
    half = width // 2
    blocks = width // LANES
    for gathered, which in ((mine, core[0]), (other, 1 - core[0])):
        peers, rows, lanes = gathered.shape
        first = gathered[:, :early, :].astype(F32).reshape(peers * early, lanes)
        second = gathered[:, early:, :].astype(F32).reshape(peers * (rows - early), lanes)
        places = ((outer, 0, first), (inner, 0, first), (inner, width, first), (coarse, 0, first))
        places += ((edge, 0, second), (source, 0, second), (target, 0, second))
        for number, (out, base, values) in enumerate(places):
            at = (number if number < 4 else number - 4) * blocks * half
            span = pl.ds(pl.multiple_of(base + which * half, half), half)
            for k in range(blocks):
                out[span, k * LANES : (k + 1) * LANES] = values[at + k * half : at + (k + 1) * half, :]


def call(kernel, outs, *args, scratch=(), core=None, **static):
    body = functools.partial(kernel, *static.values())
    specs = [pl.BlockSpec(memory_space=pltpu.VMEM)] * len(args)
    if core is not None:
        args, specs = (core,) + args, [pl.BlockSpec(memory_space=pltpu.SMEM)] + specs
    return pl.pallas_call(
        body,
        in_specs=specs,
        out_shape=[jax.ShapeDtypeStruct(shape, dtype) for shape, dtype in outs],
        scratch_shapes=[pltpu.VMEM(shape, dtype) for shape, dtype in scratch],
        compiler_params=pltpu.CompilerParams(vmem_limit_bytes=60 * 2 ** 20),
    )(*args)


def passed_along(value, axis, steps):
    count = math.prod(lax.axis_size(name) for name in axis)
    initial, last = (max(0, -steps), min(count, count - steps))
    return lax.ppermute(value, axis, [(source, source + steps) for source in range(initial, last)])


def trade_halo(blocks, flip):
    moved = []
    for number, (axis, offset) in enumerate(((ROW, 1), (ROW, -1), (COL, 1), (COL, -1))):
        moved.append(passed_along(blocks[number], axis, offset * flip))
    return moved


def trade_slots(buffer, devices):
    slots, width = buffer.shape
    shaped = buffer.reshape(devices, slots // devices, width)
    moved = lax.all_to_all(shaped, ALL, split_axis=0, concat_axis=0, tiled=True)
    return moved.reshape(slots, width)


def across(value):
    return lax.ppermute(value, "core", [(0, 1), (1, 0)])


def paired(keep, give):
    return (keep.astype(F32) + across(give).astype(F32)).astype(BF)


def trade_chips(value):
    return lax.all_to_all(value, CHIPS, split_axis=0, concat_axis=0, tiled=True)


def total(arrived):
    return jnp.sum(arrived.astype(F32), axis=0).astype(BF)


def local(
    nodes,
    cotangent,
    edge_source,
    edge_target,
    halo_lists,
    pool_owner,
    pool_table,
    source_weight,
    target_weight,
    edge_weight,
    inner_weight,
    outer_weight,
    coarse_weight,
):
    chips = math.prod(lax.axis_size(name) for name in CHIPS)
    devices = 2 * chips
    core = lax.axis_index("core").reshape(1)
    rows, width = nodes.shape
    edges = edge_source.shape[0]
    halo_rows = halo_lists.shape[2]
    extended = rows + 4 * halo_rows
    slots = pool_table.shape[1]
    coarse_rows = rows // 4
    scale = 1.0 / math.sqrt(rows * devices)
    lists = halo_lists.reshape(1, 4 * halo_rows)
    owner = pool_owner.reshape(rows // LANES, LANES)
    table = pool_table.reshape(slots // LANES, LANES)
    senders = edge_source.reshape(edges // LANES, LANES)
    receivers = edge_target.reshape(edges // LANES, LANES)
    node_block, edge_block = (rows, width), (edges, width)
    square = ((width, width), F32)
    packed = width // 2 * width // LANES

    (halo_sent,) = call(halo_kernel, [((4 * halo_rows, width), BF)], nodes, lists)
    sent_blocks = [halo_sent[k * halo_rows : (k + 1) * halo_rows] for k in range(4)]
    halo = trade_halo(sent_blocks, 1)
    slot, cot_sent, own_source, target_side = call(
        prepare_kernel,
        [((1, rows), jnp.int32), ((slots, width), BF), (node_block, BF), (node_block, BF)],
        owner, cotangent, nodes, source_weight, target_weight,
    )
    cot_arrived = trade_slots(cot_sent, devices)
    edge_hidden, edge_slope, message_slope, aggregate, node_hidden, node_slope, refined, sent = call(
        forward_kernel,
        [(edge_block, BF)] * 3 + [(node_block, BF)] * 4 + [((slots, width), BF)],
        *halo, own_source, target_side, nodes, senders, receivers, slot,
        source_weight, edge_weight, inner_weight, outer_weight,
        scratch=[((extended + rows, width), BF), (edge_block, BF), ((rows, edges), BF)],
    )
    arrived = trade_slots(sent, devices)
    members, totals, counts = call(
        members_kernel,
        [((coarse_rows, slots), BF), ((coarse_rows, width), F32), ((coarse_rows, LANES), F32)],
        cot_arrived, table,
    )
    sent, coarse, grad_coarse = call(
        coarse_kernel,
        [((slots, 2 * width), BF)] + [((coarse_rows, width), BF)] * 2,
        arrived, members, totals, counts, table, coarse_weight,
    )
    returned = trade_slots(sent, devices)
    grad_aggregate, base, keep, give = call(
        node_back_kernel,
        [(node_block, BF), (node_block, F32), ((4 * packed, LANES), BF), ((4 * packed, LANES), BF)],
        returned, slot, cotangent, nodes, aggregate, node_hidden, node_slope, coarse, grad_coarse,
        inner_weight, outer_weight,
        core=core, scale=scale,
    )
    early = paired(keep, give)
    grad_message, grad_edges, grad_sources, back = call(
        edge_back_kernel,
        [(edge_block, BF), (edge_block, BF), ((extended, width), BF), ((4 * halo_rows, width), BF)],
        senders, receivers, grad_aggregate, edge_slope, message_slope, edge_weight, source_weight,
        scratch=[((extended, edges), BF)],
    )
    early_rows = 4 * packed // chips
    early = total(trade_chips(early.reshape(chips, early_rows, LANES)))
    halo_back = trade_halo([back[k * halo_rows : (k + 1) * halo_rows] for k in range(4)], -1)
    keep, give, partial = call(
        weights_kernel,
        [((3 * packed, LANES), BF), ((3 * packed, LANES), BF), (node_block, F32)],
        receivers, edge_hidden, grad_message, grad_edges, grad_sources, *halo,
        nodes, base, source_weight, target_weight,
        scratch=[((rows, edges), BF), ((extended, width), BF)],
        core=core, scale=scale,
    )
    late = paired(keep, give)
    late_rows = 3 * packed // chips
    late = total(trade_chips(late.reshape(chips, late_rows, LANES)))
    sent = jnp.concatenate([early, late], axis=0)
    sent = jnp.broadcast_to(sent[None], (chips,) + sent.shape)
    mine = trade_chips(sent)
    (node_gradient,) = call(node_gradient_kernel, [(node_block, F32)], partial, lists, *halo_back)
    (updated,) = call(updated_kernel, [(node_block, BF)], refined, returned, slot)
    results = call(
        results_kernel,
        [square, square, square, ((2 * width, width), F32), square, square],
        mine, across(mine),
        core=core, early=early_rows,
    )
    return (updated, node_gradient, *results)


def solution(mesh):
    whole = mesh.devices.reshape(mesh.shape["row"] // 2, 2, -1, 4)
    mesh = Mesh(whole, ALL)
    in_specs = (
        P(ALL, None),
        P(ALL, None),
        P(ALL),
        P(ALL),
        P(ALL, None, None),
        P(ALL),
        P(ALL, None),
        P(),
        P(),
        P(),
        P(),
        P(),
        P(),
    )
    out_specs = (P(ALL, None), P(ALL, None), P(), P(), P(), P(), P(), P())

    return jax.shard_map(local, mesh=mesh, in_specs=in_specs, out_specs=out_specs, check_vma=False)
```

```python
import functools
import math

import jax
import jax.numpy as jnp
from jax import lax
from jax.experimental import pallas as pl
from jax.experimental.pallas import tpu as pltpu
from jax.sharding import Mesh
from jax.sharding import PartitionSpec as P


BF = jnp.bfloat16
F32 = jnp.float32
LANES = 128
CHUNK = 512
CAPACITY = 8
ROW = ("z", "core")
COL = ("x", "y")
CHIPS = ("z", "x", "y")
ALL = ROW + COL


def dot(first, second):
    return jnp.dot(first, second, preferred_element_type=F32)


def left_dot(first, second):
    return lax.dot_general(
        first, second, (((0,), (0,)), ((), ())), preferred_element_type=F32
    )


def right_dot(first, second):
    return lax.dot_general(
        first, second, (((1,), (1,)), ((), ())), preferred_element_type=F32
    )


def iota(shape, axis):
    return lax.broadcasted_iota(jnp.int32, shape, axis)


def column(row):
    square = (LANES, LANES)
    eye = iota(square, 0) == iota(square, 1)
    spread = jnp.broadcast_to(row.astype(F32), square)
    return jnp.sum(jnp.where(eye, spread, 0.0), axis=1, keepdims=True).astype(jnp.int32)


def hot(mask):
    return jnp.where(mask, 1.0, 0.0).astype(BF)


def wide_column(row):
    return jnp.concatenate(
        [column(row[:, k : k + LANES]) for k in range(0, row.shape[1], LANES)], axis=0
    )


def wide_row(ref):
    return jnp.concatenate([ref[k : k + 1, :] for k in range(ref.shape[0])], axis=1)


def gates(value):
    sigma = 0.5 * jnp.tanh(0.5 * value) + 0.5
    active = value * sigma
    return active, sigma + active * (1.0 - sigma)


def halo_kernel(nodes, lists, out):
    picks = hot(column(lists[...]) == iota((LANES, nodes.shape[0]), 1))
    out[...] = dot(picks, nodes[...]).astype(BF)


def prepare_kernel(owner, nodes, source_weight, target_weight, slot_out, own_source, target_side):
    rows = nodes.shape[0]
    owner_row = wide_row(owner)
    owner_column = wide_column(owner_row)
    square = (rows, rows)
    before = (owner_column == owner_row) & (iota(square, 0) < iota(square, 1))
    rank = jnp.sum(jnp.where(before, 1.0, 0.0), axis=0, keepdims=True).astype(jnp.int32)
    slot_out[...] = owner_row * CAPACITY + rank
    own_source[...] = dot(nodes[...], source_weight[...]).astype(BF)
    target_side[...] = dot(nodes[...], target_weight[...]).astype(BF)


def chunk(turn):
    return slice(turn * CHUNK, (turn + 1) * CHUNK)


def forward_kernel(
    halo_0, halo_1, halo_2, halo_3, own_source, target_side, nodes, cotangent, edge_source, edge_target, slot,
    source_weight, edge_weight, inner_far, outer_far,
    edge_hidden, edge_slope, message_slope, aggregate, node_hidden, node_slope, refined, sent,
    sides, active, spread, inner_weight, outer_weight, hidden_kept, slope_kept, message_kept, weight_sems, sems,
):
    fetches = [
        pltpu.make_async_copy(inner_far, inner_weight, weight_sems.at[0]),
        pltpu.make_async_copy(outer_far, outer_weight, weight_sems.at[1]),
    ]
    for fetch in fetches:
        fetch.start()
    rows, width = nodes.shape
    extended = rows + LANES
    edges = hidden_kept.shape[0]
    sides[:rows, :] = own_source[...]
    halo = jnp.concatenate([halo_0[...], halo_1[...], halo_2[...], halo_3[...]], axis=0)
    sides[rows:extended, :] = dot(halo, source_weight[...]).astype(BF)
    sides[extended:, :] = target_side[...]
    group = CHUNK // LANES
    stores = []
    for turn in range(edges // CHUNK):
        span = chunk(turn)
        picks = []
        for at in range(turn * group, (turn + 1) * group):
            senders = edge_source[at : at + 1, :]
            receivers = edge_target[at : at + 1, :]
            sender_hot = hot(column(senders) == iota((LANES, extended), 1))
            receiver_hot = hot(column(receivers) == iota((LANES, rows), 1))
            picks.append(jnp.concatenate([sender_hot, receiver_hot], axis=1))
            spread[:, at * LANES : (at + 1) * LANES] = hot(iota((rows, LANES), 0) == receivers)
        hidden, slope = gates(dot(jnp.concatenate(picks, axis=0), sides[...]))
        hidden = hidden.astype(BF)
        hidden_kept[span, :] = hidden
        slope_kept[span, :] = slope.astype(BF)
        message, slope = gates(dot(hidden, edge_weight[...]))
        active[span, :] = message.astype(BF)
        message_kept[span, :] = slope.astype(BF)
        pairs = ((hidden_kept, edge_hidden), (slope_kept, edge_slope), (message_kept, message_slope))
        for number, (kept, out) in enumerate(pairs):
            stores.append(pltpu.make_async_copy(kept.at[span, :], out.at[span, :], sems.at[number, turn]))
            stores[-1].start()
    gathered = dot(spread[...], active[...]).astype(BF)
    aggregate[...] = gathered
    for fetch in fetches:
        fetch.wait()
    linear = dot(nodes[...], inner_weight[:width, :]) + dot(gathered, inner_weight[width:, :])
    hidden, slope = gates(linear)
    hidden = hidden.astype(BF)
    node_hidden[...] = hidden
    node_slope[...] = slope.astype(BF)
    result = (nodes[...].astype(F32) + dot(hidden, outer_weight[...])).astype(BF)
    refined[...] = result
    place = hot(iota((sent.shape[0], rows), 0) == slot[...])
    sent[:, :width] = dot(place, result).astype(BF)
    sent[:, width:] = dot(place, cotangent[...]).astype(BF)
    for store in stores:
        store.wait()


def members_kernel(table, members, picks, counts):
    coarse = members.shape[0]
    row = wide_row(table)
    inside = iota((coarse, row.shape[1]), 0) == row
    ones = jnp.where(inside, 1.0, 0.0)
    members[...] = ones.astype(BF)
    count = jnp.maximum(jnp.sum(ones, axis=1, keepdims=True), 1.0)
    counts[...] = jnp.broadcast_to(count, counts.shape)
    picks[...] = hot(wide_column(row) == iota((row.shape[1], coarse), 1))


def coarse_kernel(arrived, members, picks, counts, weight, out, coarse_out, grad_out):
    width = weight.shape[0]
    count = counts[:, :1]
    totals = dot(members[...], arrived[...])
    coarse = (totals[:, :width] / count).astype(BF)
    coarse_out[...] = coarse
    active, slope = gates(dot(coarse, weight[...]))
    grad = (totals[:, width:] * slope).astype(BF)
    grad_out[...] = grad
    share = (right_dot(grad, weight[...]) / count).astype(BF)
    out[:, :width] = dot(picks[...], share).astype(BF)
    out[:, width:] = dot(picks[...], active.astype(BF)).astype(BF)


def half_of(ref, half):
    columns = ref.shape[1] // 2
    return ref[:, pl.ds(pl.multiple_of(half * columns, columns), columns)]


def pack(out, at, value):
    rows, width = value.shape
    for k in range(width // LANES):
        out[at * width // LANES + k * rows : at * width // LANES + (k + 1) * rows, :] = value[
            :, k * LANES : (k + 1) * LANES
        ].astype(BF)


def halves(scale, core, keep, give, pairs):
    at = 0
    for first, second in pairs:
        for out, half in ((keep, core[0]), (give, 1 - core[0])):
            pack(out, at, left_dot(half_of(first, half), second) * scale)
        at += first.shape[1] // 2


def node_back_kernel(
    scale, core, returned, slot, cotangent, nodes, aggregate, node_hidden, node_slope, coarse, grad_coarse,
    inner_weight, outer_weight,
    grad_aggregate, grad_hidden, keep, give,
):
    rows, width = nodes.shape
    picks = hot(wide_column(slot[...]) == iota((rows, returned.shape[0]), 1))
    grad = cotangent[...].astype(F32) + dot(picks, returned[:, :width])
    low = grad.astype(BF)
    hidden = (right_dot(low, outer_weight[...]) * node_slope[...].astype(F32)).astype(BF)
    grad_hidden[...] = hidden
    grad_aggregate[...] = right_dot(hidden, inner_weight[width:, :]).astype(BF)
    pairs = ((node_hidden, low), (nodes, hidden), (aggregate, hidden), (coarse, grad_coarse[...]))
    halves(scale, core, keep, give, pairs)


def edge_back_kernel(
    scale, core, edge_source, edge_target, grad_aggregate, halo_0, halo_1, halo_2, halo_3, nodes, edge_weight,
    source_weight, edge_slope, message_slope, edge_hidden,
    keep, give, grad_sources, grad_targets, back,
    slope_kept, message_kept, hidden_kept, grad_message, grad_edges, source_spread, target_spread, extended, sems,
):
    rows, _ = nodes.shape
    table = grad_sources.shape[0]
    edges = slope_kept.shape[0]
    turns = edges // CHUNK
    group = CHUNK // LANES
    fetches = []
    for turn in range(turns):
        span = chunk(turn)
        for number, (far, kept) in enumerate(((message_slope, message_kept), (edge_slope, slope_kept))):
            fetches.append(pltpu.make_async_copy(far.at[span, :], kept.at[span, :], sems.at[number, turn]))
    fetches.append(pltpu.make_async_copy(edge_hidden, hidden_kept, sems.at[2, 0]))
    for fetch in fetches:
        fetch.start()
    extended[:rows, :] = nodes[...]
    extended[rows:, :] = jnp.concatenate([halo_0[...], halo_1[...], halo_2[...], halo_3[...]], axis=0)
    for turn in range(turns):
        span = chunk(turn)
        picks = []
        for at in range(turn * group, (turn + 1) * group):
            senders = edge_source[at : at + 1, :]
            receivers = edge_target[at : at + 1, :]
            lanes = slice(at * LANES, (at + 1) * LANES)
            picks.append(hot(column(receivers) == iota((LANES, rows), 1)))
            source_spread[:, lanes] = hot(iota((table, LANES), 0) == senders)
            target_spread[:, lanes] = hot(iota((rows, LANES), 0) == receivers)
        taken = dot(jnp.concatenate(picks, axis=0), grad_aggregate[...])
        fetches[2 * turn].wait()
        message = (taken * message_kept[span, :].astype(F32)).astype(BF)
        grad_message[span, :] = message
        fetches[2 * turn + 1].wait()
        grad = right_dot(message, edge_weight[...]) * slope_kept[span, :].astype(F32)
        grad_edges[span, :] = grad.astype(BF)
    sources = dot(source_spread[...], grad_edges[...]).astype(BF)
    targets = dot(target_spread[...], grad_edges[...]).astype(BF)
    grad_sources[...] = sources
    grad_targets[...] = targets
    back[...] = right_dot(sources[rows:, :], source_weight[...]).astype(BF)
    fetches[-1].wait()
    pairs = ((hidden_kept, grad_message[...]), (extended, sources), (nodes, targets))
    halves(scale, core, keep, give, pairs)


def finish_kernel(
    returned, slot, cotangent, refined, grad_hidden, grad_sources, grad_targets, lists,
    back_0, back_1, back_2, back_3, inner_weight, source_weight, target_weight,
    updated, node_gradient,
):
    rows, width = refined.shape
    picks = hot(wide_column(slot[...]) == iota((rows, returned.shape[0]), 1))
    updated[...] = (refined[...].astype(F32) + dot(picks, returned[:, width:])).astype(BF)
    back = jnp.concatenate([back_0[...], back_1[...], back_2[...], back_3[...]], axis=0)
    places = hot(iota((rows, LANES), 0) == lists[...])
    node_gradient[...] = (
        cotangent[...].astype(F32)
        + dot(picks, returned[:, :width])
        + right_dot(grad_hidden[...], inner_weight[:width, :])
        + right_dot(grad_targets[...], target_weight[...])
        + right_dot(grad_sources[:rows, :], source_weight[...])
        + dot(places, back)
    )


def results_kernel(early, other, core, gathered, *refs):
    outs, wide, sems = refs[-8:-2], refs[-2], refs[-1]
    source, target, edge, inner, outer, coarse = outs
    which = 1 - core[0] if other else core[0]
    width = wide.shape[1]
    half = width // 2
    blocks = width // LANES
    peers, rows, lanes = gathered.shape
    first = gathered[:, :early, :].astype(F32).reshape(peers * early, lanes)
    second = gathered[:, early:, :].astype(F32).reshape(peers * (rows - early), lanes)
    places = ((outer, 0, first, 0), (inner, 0, first, 1), (inner, width, first, 2), (coarse, 0, first, 3))
    places += ((edge, 0, second, 0), (source, 0, second, 1), (target, 0, second, 2))
    stores = []
    for number, (out, base, values, at) in enumerate(places):
        own = slice(number * half, (number + 1) * half)
        for k in range(blocks):
            start = (at * blocks + k) * half
            wide[own, k * LANES : (k + 1) * LANES] = values[start : start + half, :]
        span = pl.ds(pl.multiple_of(base + which * half, half), half)
        stores.append(pltpu.make_async_copy(wide.at[own, :], out.at[span, :], sems.at[number]))
        stores[-1].start()
    for store in stores:
        store.wait()


def call(kernel, outs, *args, far_in=0, far_out=0, scratch=(), sems=(), core=None, aliases=0, **static):
    body = functools.partial(kernel, *static.values())
    near, far = pl.BlockSpec(memory_space=pltpu.VMEM), pl.BlockSpec(memory_space=pl.ANY)
    specs = [near] * (len(args) - far_in) + [far] * far_in
    if core is not None:
        args, specs = (core,) + args, [pl.BlockSpec(memory_space=pltpu.SMEM)] + specs
    return pl.pallas_call(
        body,
        in_specs=specs,
        out_specs=[far] * far_out + [near] * (len(outs) - far_out),
        out_shape=[jax.ShapeDtypeStruct(shape, dtype) for shape, dtype in outs],
        scratch_shapes=[pltpu.VMEM(shape, dtype) for shape, dtype in scratch]
        + [pltpu.SemaphoreType.DMA(shape) for shape in sems],
        compiler_params=pltpu.CompilerParams(vmem_limit_bytes=60 * 2 ** 20),
        input_output_aliases={len(args) - aliases + k: k for k in range(aliases)},
    )(*args)


def passed_along(value, axis, steps):
    count = math.prod(lax.axis_size(name) for name in axis)
    initial, last = (max(0, -steps), min(count, count - steps))
    return lax.ppermute(value, axis, [(source, source + steps) for source in range(initial, last)])


def trade_halo(blocks, flip):
    moved = []
    for number, (axis, offset) in enumerate(((ROW, 1), (ROW, -1), (COL, 1), (COL, -1))):
        moved.append(passed_along(blocks[number], axis, offset * flip))
    return moved


def trade_slots(buffer, devices):
    slots, width = buffer.shape
    shaped = buffer.reshape(devices, slots // devices, width)
    moved = lax.all_to_all(shaped, ALL, split_axis=0, concat_axis=0, tiled=True)
    return moved.reshape(slots, width)


def across(value):
    return lax.ppermute(value, "core", [(0, 1), (1, 0)])


def paired(keep, give):
    return (keep.astype(F32) + across(give).astype(F32)).astype(BF)


def trade_chips(value):
    return lax.all_to_all(value, CHIPS, split_axis=0, concat_axis=0, tiled=True)


def total(arrived):
    return jnp.sum(arrived.astype(F32), axis=0).astype(BF)


def local(
    nodes,
    cotangent,
    edge_source,
    edge_target,
    halo_lists,
    pool_owner,
    pool_table,
    source_weight,
    target_weight,
    edge_weight,
    inner_weight,
    outer_weight,
    coarse_weight,
):
    chips = math.prod(lax.axis_size(name) for name in CHIPS)
    devices = 2 * chips
    core = lax.axis_index("core").reshape(1)
    rows, width = nodes.shape
    edges = edge_source.shape[0]
    halo_rows = halo_lists.shape[2]
    extended = rows + 4 * halo_rows
    slots = pool_table.shape[1]
    coarse_rows = rows // 4
    scale = 1.0 / math.sqrt(rows * devices)
    lists = halo_lists.reshape(1, 4 * halo_rows)
    owner = pool_owner.reshape(rows // LANES, LANES)
    table = pool_table.reshape(slots // LANES, LANES)
    senders = edge_source.reshape(edges // LANES, LANES)
    receivers = edge_target.reshape(edges // LANES, LANES)
    node_block, edge_block = (rows, width), (edges, width)
    square = ((width, width), F32)
    packed = width // 2 * width // LANES

    (halo_sent,) = call(halo_kernel, [((4 * halo_rows, width), BF)], nodes, lists)
    sent_blocks = [halo_sent[k * halo_rows : (k + 1) * halo_rows] for k in range(4)]
    halo = trade_halo(sent_blocks, 1)
    slot, own_source, target_side = call(
        prepare_kernel,
        [((1, rows), jnp.int32), (node_block, BF), (node_block, BF)],
        owner, nodes, source_weight, target_weight,
    )
    edge_hidden, edge_slope, message_slope, aggregate, node_hidden, node_slope, refined, sent = call(
        forward_kernel,
        [(edge_block, BF)] * 3 + [(node_block, BF)] * 4 + [((slots, 2 * width), BF)],
        *halo, own_source, target_side, nodes, cotangent, senders, receivers, slot,
        source_weight, edge_weight, inner_weight, outer_weight,
        far_in=2, far_out=3,
        scratch=[((extended + rows, width), BF), (edge_block, BF), ((rows, edges), BF)]
        + [((2 * width, width), BF), ((width, width), BF)] + [(edge_block, BF)] * 3,
        sems=[(2,), (3, edges // CHUNK)],
    )
    arrived = trade_slots(sent, devices)
    members, picks, counts = call(
        members_kernel,
        [((coarse_rows, slots), BF), ((slots, coarse_rows), BF), ((coarse_rows, LANES), F32)],
        table,
    )
    sent, coarse, grad_coarse = call(
        coarse_kernel,
        [((slots, 2 * width), BF)] + [((coarse_rows, width), BF)] * 2,
        arrived, members, picks, counts, coarse_weight,
    )
    returned = trade_slots(sent, devices)
    grad_aggregate, grad_hidden, keep, give = call(
        node_back_kernel,
        [(node_block, BF), (node_block, BF), ((4 * packed, LANES), BF), ((4 * packed, LANES), BF)],
        returned, slot, cotangent, nodes, aggregate, node_hidden, node_slope, coarse, grad_coarse,
        inner_weight, outer_weight,
        core=core, scale=scale,
    )
    early = paired(keep, give)
    early_rows = 4 * packed // chips
    early = total(trade_chips(early.reshape(chips, early_rows, LANES)))
    keep, give, grad_sources, grad_targets, back = call(
        edge_back_kernel,
        [((3 * packed, LANES), BF)] * 2 + [((extended, width), BF), (node_block, BF), ((4 * halo_rows, width), BF)],
        senders, receivers, grad_aggregate, *halo, nodes, edge_weight, source_weight,
        edge_slope, message_slope, edge_hidden,
        far_in=3,
        scratch=[(edge_block, BF)] * 5 + [((extended, edges), BF), ((rows, edges), BF), ((extended, width), BF)],
        sems=[(3, edges // CHUNK)],
        core=core, scale=scale,
    )
    halo_back = trade_halo([back[k * halo_rows : (k + 1) * halo_rows] for k in range(4)], -1)
    late = paired(keep, give)
    late_rows = 3 * packed // chips
    late = total(trade_chips(late.reshape(chips, late_rows, LANES)))
    sent = jnp.concatenate([early, late], axis=0)
    sent = jnp.broadcast_to(sent[None], (chips,) + sent.shape)
    mine = trade_chips(sent)
    updated, node_gradient = call(
        finish_kernel,
        [(node_block, BF), (node_block, F32)],
        returned, slot, cotangent, refined, grad_hidden, grad_sources, grad_targets, lists, *halo_back,
        inner_weight, source_weight, target_weight,
    )
    shapes = [square, square, square, ((2 * width, width), F32), square, square]
    buffers = {"scratch": [((7 * width // 2, width), F32)], "sems": [(7,)], "far_out": 6, "core": core}
    results = call(results_kernel, shapes, mine, **buffers, early=early_rows, other=False)
    results = call(
        results_kernel, shapes, across(mine), *results, far_in=6, aliases=6,
        **buffers, early=early_rows, other=True,
    )
    return (updated, node_gradient, *results)


def solution(mesh):
    whole = mesh.devices.reshape(mesh.shape["row"] // 2, 2, -1, 4)
    mesh = Mesh(whole, ALL)
    in_specs = (
        P(ALL, None),
        P(ALL, None),
        P(ALL),
        P(ALL),
        P(ALL, None, None),
        P(ALL),
        P(ALL, None),
        P(),
        P(),
        P(),
        P(),
        P(),
        P(),
    )
    out_specs = (P(ALL, None), P(ALL, None), P(), P(), P(), P(), P(), P())

    return jax.shard_map(local, mesh=mesh, in_specs=in_specs, out_specs=out_specs, check_vma=False)
```

```python
import functools
import math

import jax
import jax.numpy as jnp
from jax import lax
from jax.experimental import pallas as pl
from jax.experimental.pallas import tpu as pltpu
from jax.sharding import Mesh
from jax.sharding import PartitionSpec as P


BF = jnp.bfloat16
F32 = jnp.float32
LANES = 128
CHUNK = 1024
CAPACITY = 8
ROW = ("z", "core")
COL = ("x", "y")
CHIPS = ("z", "x", "y")
ALL = ROW + COL


def dot(first, second):
    return jnp.dot(first, second, preferred_element_type=F32)


def left_dot(first, second):
    return lax.dot_general(
        first, second, (((0,), (0,)), ((), ())), preferred_element_type=F32
    )


def right_dot(first, second):
    return lax.dot_general(
        first, second, (((1,), (1,)), ((), ())), preferred_element_type=F32
    )


def iota(shape, axis):
    return lax.broadcasted_iota(jnp.int32, shape, axis)


def column(row):
    square = (row.shape[1],) * 2
    eye = iota(square, 0) == iota(square, 1)
    spread = jnp.broadcast_to(row.astype(F32), square)
    return jnp.sum(jnp.where(eye, spread, 0.0), axis=1, keepdims=True).astype(jnp.int32)


def hot(mask):
    return jnp.where(mask, 1.0, 0.0).astype(BF)


def wide_column(row):
    return jnp.concatenate(
        [column(row[:, k : k + LANES]) for k in range(0, row.shape[1], LANES)], axis=0
    )


def wide_row(ref):
    return jnp.concatenate([ref[k : k + 1, :] for k in range(ref.shape[0])], axis=1)


def gates(value):
    sigma = 0.5 * jnp.tanh(0.5 * value) + 0.5
    active = value * sigma
    return active, sigma + active * (1.0 - sigma)


def sent_order(where):
    return where[0], 1 - where[0], 2 + where[1], 3 - where[1]


def received_order(where):
    return 1 - where[0], where[0], 3 - where[1], 2 + where[1]


def block(at, base, rows):
    return pl.ds(pl.multiple_of(base + at * rows, rows), rows)


def halo_picks(where, lists, rows):
    length = lists.shape[2]
    columns = [column(lists[0, pl.ds(at, 1), :]) for at in sent_order(where)]
    return jnp.concatenate([hot(each == iota((length, rows), 1)) for each in columns], axis=0)


def halo_kernel(where, nodes, lists, *outs):
    picked = dot(halo_picks(where, lists, nodes.shape[0]), nodes[...]).astype(BF)
    rows = outs[0].shape[0]
    for number, out in enumerate(outs):
        out[...] = picked[number * rows : (number + 1) * rows, :]


def prepare_kernel(owner, nodes, source_weight, target_weight, slot_out, own_source, target_side):
    rows = nodes.shape[0]
    owner_row = wide_row(owner)
    owner_column = wide_column(owner_row)
    square = (rows, rows)
    before = (owner_column == owner_row) & (iota(square, 0) < iota(square, 1))
    rank = jnp.sum(jnp.where(before, 1.0, 0.0), axis=0, keepdims=True).astype(jnp.int32)
    slot_out[...] = owner_row * CAPACITY + rank
    own_source[...] = dot(nodes[...], source_weight[...]).astype(BF)
    target_side[...] = dot(nodes[...], target_weight[...]).astype(BF)


def chunk(turn):
    return slice(turn * CHUNK, (turn + 1) * CHUNK)


def forward_kernel(
    where, halo_0, halo_1, halo_2, halo_3, own_source, target_side, nodes, cotangent, edge_source, edge_target, slot,
    source_weight, edge_weight, inner_far, outer_far,
    edge_hidden, edge_slope, message_slope, aggregate, node_hidden, node_slope, refined, sent,
    sides, active, spread, inner_weight, outer_weight, hidden_kept, slope_kept, message_kept, weight_sems, sems,
):
    fetches = [
        pltpu.make_async_copy(inner_far, inner_weight, weight_sems.at[0]),
        pltpu.make_async_copy(outer_far, outer_weight, weight_sems.at[1]),
    ]
    for fetch in fetches:
        fetch.start()
    rows, width = nodes.shape
    extended = rows + LANES
    edges = hidden_kept.shape[0]
    sides[:rows, :] = own_source[...]
    halo = jnp.concatenate([halo_0[...], halo_1[...], halo_2[...], halo_3[...]], axis=0)
    halo = dot(halo, source_weight[...]).astype(BF)
    length = halo_0.shape[0]
    for number, at in enumerate(received_order(where)):
        sides[block(at, rows, length), :] = halo[number * length : (number + 1) * length, :]
    sides[extended:, :] = target_side[...]
    group = CHUNK // LANES
    stores = []
    for turn in range(edges // CHUNK):
        span = chunk(turn)
        picks = []
        for at in range(turn * group, (turn + 1) * group):
            senders = edge_source[at : at + 1, :]
            receivers = edge_target[at : at + 1, :]
            sender_hot = hot(column(senders) == iota((LANES, extended), 1))
            receiver_hot = hot(column(receivers) == iota((LANES, rows), 1))
            picks.append(jnp.concatenate([sender_hot, receiver_hot], axis=1))
            spread[:, at * LANES : (at + 1) * LANES] = hot(iota((rows, LANES), 0) == receivers)
        hidden, slope = gates(dot(jnp.concatenate(picks, axis=0), sides[...]))
        hidden = hidden.astype(BF)
        hidden_kept[span, :] = hidden
        slope_kept[span, :] = slope.astype(BF)
        message, slope = gates(dot(hidden, edge_weight[...]))
        active[span, :] = message.astype(BF)
        message_kept[span, :] = slope.astype(BF)
        pairs = ((hidden_kept, edge_hidden), (slope_kept, edge_slope), (message_kept, message_slope))
        for number, (kept, out) in enumerate(pairs):
            stores.append(pltpu.make_async_copy(kept.at[span, :], out.at[span, :], sems.at[number, turn]))
            stores[-1].start()
    gathered = dot(spread[...], active[...]).astype(BF)
    aggregate[...] = gathered
    for fetch in fetches:
        fetch.wait()
    linear = dot(nodes[...], inner_weight[:width, :]) + dot(gathered, inner_weight[width:, :])
    hidden, slope = gates(linear)
    hidden = hidden.astype(BF)
    node_hidden[...] = hidden
    node_slope[...] = slope.astype(BF)
    result = (nodes[...].astype(F32) + dot(hidden, outer_weight[...])).astype(BF)
    refined[...] = result
    place = hot(iota((sent.shape[0], rows), 0) == slot[...])
    sent[:, :width] = dot(place, result).astype(BF)
    sent[:, width:] = dot(place, cotangent[...]).astype(BF)
    for store in stores:
        store.wait()


def members_kernel(table, members, picks, counts):
    coarse = members.shape[0]
    row = wide_row(table)
    inside = iota((coarse, row.shape[1]), 0) == row
    ones = jnp.where(inside, 1.0, 0.0)
    members[...] = ones.astype(BF)
    count = jnp.maximum(jnp.sum(ones, axis=1, keepdims=True), 1.0)
    counts[...] = jnp.broadcast_to(count, counts.shape)
    picks[...] = hot(wide_column(row) == iota((row.shape[1], coarse), 1))


def coarse_kernel(arrived, members, picks, counts, weight, out, coarse_out, grad_out):
    width = weight.shape[0]
    count = counts[:, :1]
    totals = dot(members[...], arrived[...])
    coarse = (totals[:, :width] / count).astype(BF)
    coarse_out[...] = coarse
    active, slope = gates(dot(coarse, weight[...]))
    grad = (totals[:, width:] * slope).astype(BF)
    grad_out[...] = grad
    share = (right_dot(grad, weight[...]) / count).astype(BF)
    out[:, :width] = dot(picks[...], share).astype(BF)
    out[:, width:] = dot(picks[...], active.astype(BF)).astype(BF)


def half_of(ref, half):
    columns = ref.shape[1] // 2
    return ref[:, pl.ds(pl.multiple_of(half * columns, columns), columns)]


def pack(out, at, value):
    rows, width = value.shape
    for k in range(width // LANES):
        out[at * width // LANES + k * rows : at * width // LANES + (k + 1) * rows, :] = value[
            :, k * LANES : (k + 1) * LANES
        ].astype(BF)


def halves(scale, where, keep, give, pairs):
    at = 0
    for first, second in pairs:
        for out, half in ((keep, where[0]), (give, 1 - where[0])):
            pack(out, at, left_dot(half_of(first, half), second) * scale)
        at += first.shape[1] // 2


def node_back_kernel(
    scale, where, returned, slot, cotangent, nodes, aggregate, node_hidden, node_slope, coarse, grad_coarse,
    inner_weight, outer_weight,
    grad_aggregate, grad_hidden, keep, give,
):
    rows, width = nodes.shape
    picks = hot(wide_column(slot[...]) == iota((rows, returned.shape[0]), 1))
    grad = cotangent[...].astype(F32) + dot(picks, returned[:, :width])
    low = grad.astype(BF)
    hidden = (right_dot(low, outer_weight[...]) * node_slope[...].astype(F32)).astype(BF)
    grad_hidden[...] = hidden
    grad_aggregate[...] = right_dot(hidden, inner_weight[width:, :]).astype(BF)
    pairs = ((node_hidden, low), (nodes, hidden), (aggregate, hidden), (coarse, grad_coarse[...]))
    halves(scale, where, keep, give, pairs)


def edge_back_kernel(
    scale, where, edge_source, edge_target, grad_aggregate, halo_0, halo_1, halo_2, halo_3, nodes, edge_weight,
    source_weight, edge_slope, message_slope, edge_hidden,
    keep, give, grad_sources, grad_targets, back_0, back_1, back_2, back_3,
    slope_kept, message_kept, hidden_kept, grad_message, grad_edges, source_spread, target_spread, extended, sems,
):
    rows, _ = nodes.shape
    table = grad_sources.shape[0]
    edges = slope_kept.shape[0]
    turns = edges // CHUNK
    group = CHUNK // LANES
    fetches = []
    for turn in range(turns):
        span = chunk(turn)
        for number, (far, kept) in enumerate(((message_slope, message_kept), (edge_slope, slope_kept))):
            fetches.append(pltpu.make_async_copy(far.at[span, :], kept.at[span, :], sems.at[number, turn]))
    fetches.append(pltpu.make_async_copy(edge_hidden, hidden_kept, sems.at[2, 0]))
    for fetch in fetches:
        fetch.start()
    extended[:rows, :] = nodes[...]
    length = halo_0.shape[0]
    received = received_order(where)
    for at, halo in zip(received, (halo_0, halo_1, halo_2, halo_3)):
        extended[block(at, rows, length), :] = halo[...]
    for turn in range(turns):
        span = chunk(turn)
        picks = []
        for at in range(turn * group, (turn + 1) * group):
            senders = edge_source[at : at + 1, :]
            receivers = edge_target[at : at + 1, :]
            lanes = slice(at * LANES, (at + 1) * LANES)
            picks.append(hot(column(receivers) == iota((LANES, rows), 1)))
            source_spread[:, lanes] = hot(iota((table, LANES), 0) == senders)
            target_spread[:, lanes] = hot(iota((rows, LANES), 0) == receivers)
        taken = dot(jnp.concatenate(picks, axis=0), grad_aggregate[...])
        fetches[2 * turn].wait()
        message = (taken * message_kept[span, :].astype(F32)).astype(BF)
        grad_message[span, :] = message
        fetches[2 * turn + 1].wait()
        grad = right_dot(message, edge_weight[...]) * slope_kept[span, :].astype(F32)
        grad_edges[span, :] = grad.astype(BF)
    sources = dot(source_spread[...], grad_edges[...]).astype(BF)
    targets = dot(target_spread[...], grad_edges[...]).astype(BF)
    grad_sources[...] = sources
    grad_targets[...] = targets
    back = jnp.concatenate([grad_sources[block(at, rows, length), :] for at in received], axis=0)
    back = right_dot(back, source_weight[...]).astype(BF)
    for number, out in enumerate((back_0, back_1, back_2, back_3)):
        out[...] = back[number * length : (number + 1) * length, :]
    fetches[-1].wait()
    pairs = ((hidden_kept, grad_message[...]), (extended, sources), (nodes, targets))
    halves(scale, where, keep, give, pairs)


def finish_kernel(
    where, returned, slot, cotangent, refined, grad_hidden, grad_sources, grad_targets, lists,
    back_0, back_1, back_2, back_3, inner_weight, source_weight, target_weight,
    updated, node_gradient,
):
    rows, width = refined.shape
    picks = hot(wide_column(slot[...]) == iota((rows, returned.shape[0]), 1))
    updated[...] = (refined[...].astype(F32) + dot(picks, returned[:, width:])).astype(BF)
    back = jnp.concatenate([back_0[...], back_1[...], back_2[...], back_3[...]], axis=0)
    places = halo_picks(where, lists, rows)
    node_gradient[...] = (
        cotangent[...].astype(F32)
        + dot(picks, returned[:, :width])
        + right_dot(grad_hidden[...], inner_weight[:width, :])
        + right_dot(grad_targets[...], target_weight[...])
        + right_dot(grad_sources[:rows, :], source_weight[...])
        + left_dot(places, back)
    )


def results_kernel(early, other, where, gathered, *refs):
    outs, wide, sems = refs[-8:-2], refs[-2], refs[-1]
    source, target, edge, inner, outer, coarse = outs
    which = 1 - where[0] if other else where[0]
    width = wide.shape[1]
    half = width // 2
    blocks = width // LANES
    peers, rows, lanes = gathered.shape
    first = gathered[:, :early, :].astype(F32).reshape(peers * early, lanes)
    second = gathered[:, early:, :].astype(F32).reshape(peers * (rows - early), lanes)
    places = ((outer, 0, first, 0), (inner, 0, first, 1), (inner, width, first, 2), (coarse, 0, first, 3))
    places += ((edge, 0, second, 0), (source, 0, second, 1), (target, 0, second, 2))
    stores = []
    for number, (out, base, values, at) in enumerate(places):
        own = slice(number * half, (number + 1) * half)
        for k in range(blocks):
            start = (at * blocks + k) * half
            wide[own, k * LANES : (k + 1) * LANES] = values[start : start + half, :]
        span = pl.ds(pl.multiple_of(base + which * half, half), half)
        stores.append(pltpu.make_async_copy(wide.at[own, :], out.at[span, :], sems.at[number]))
        stores[-1].start()
    for store in stores:
        store.wait()


def call(kernel, outs, *args, far_in=0, far_out=0, scratch=(), sems=(), where=None, aliases=0, **static):
    body = functools.partial(kernel, *static.values())
    near, far = pl.BlockSpec(memory_space=pltpu.VMEM), pl.BlockSpec(memory_space=pl.ANY)
    specs = [near] * (len(args) - far_in) + [far] * far_in
    if where is not None:
        args, specs = (where,) + args, [pl.BlockSpec(memory_space=pltpu.SMEM)] + specs
    return pl.pallas_call(
        body,
        in_specs=specs,
        out_specs=[far] * far_out + [near] * (len(outs) - far_out),
        out_shape=[jax.ShapeDtypeStruct(shape, dtype) for shape, dtype in outs],
        scratch_shapes=[pltpu.VMEM(shape, dtype) for shape, dtype in scratch]
        + [pltpu.SemaphoreType.DMA(shape) for shape in sems],
        compiler_params=pltpu.CompilerParams(vmem_limit_bytes=32 * 2 ** 20),
        input_output_aliases={len(args) - aliases + k: k for k in range(aliases)},
    )(*args)


def swapped(value, axis, first):
    count = math.prod(lax.axis_size(name) for name in axis)
    lower = range(first, count - 1, 2)
    pairs = [(at, at + 1) for at in lower] + [(at + 1, at) for at in lower]
    return lax.ppermute(value, axis, pairs)


def trade_halo(blocks):
    moved = []
    for number, (axis, first) in enumerate(((ROW, 0), (ROW, 1), (COL, 0), (COL, 1))):
        moved.append(swapped(blocks[number], axis, first))
    return moved


def trade_slots(buffer, devices):
    slots, width = buffer.shape
    shaped = buffer.reshape(devices, slots // devices, width)
    moved = lax.all_to_all(shaped, ALL, split_axis=0, concat_axis=0, tiled=True)
    return moved.reshape(slots, width)


def across(value):
    return lax.ppermute(value, "core", [(0, 1), (1, 0)])


def paired(keep, give):
    return (keep.astype(F32) + across(give).astype(F32)).astype(BF)


def trade_chips(value):
    return lax.all_to_all(value, CHIPS, split_axis=0, concat_axis=0, tiled=True)


def total(arrived):
    return jnp.sum(arrived.astype(F32), axis=0).astype(BF)


def local(
    nodes,
    cotangent,
    edge_source,
    edge_target,
    halo_lists,
    pool_owner,
    pool_table,
    source_weight,
    target_weight,
    edge_weight,
    inner_weight,
    outer_weight,
    coarse_weight,
):
    chips = math.prod(lax.axis_size(name) for name in CHIPS)
    devices = 2 * chips
    where = jnp.stack([lax.axis_index("core"), lax.axis_index("y") % 2])
    rows, width = nodes.shape
    edges = edge_source.shape[0]
    halo_rows = halo_lists.shape[2]
    extended = rows + 4 * halo_rows
    slots = pool_table.shape[1]
    coarse_rows = rows // 4
    scale = 1.0 / math.sqrt(rows * devices)
    owner = pool_owner.reshape(rows // LANES, LANES)
    table = pool_table.reshape(slots // LANES, LANES)
    senders = edge_source.reshape(edges // LANES, LANES)
    receivers = edge_target.reshape(edges // LANES, LANES)
    node_block, edge_block = (rows, width), (edges, width)
    square = ((width, width), F32)
    packed = width // 2 * width // LANES

    halo_blocks = [((halo_rows, width), BF)] * 4
    halo = trade_halo(call(halo_kernel, halo_blocks, nodes, halo_lists, where=where))
    slot, own_source, target_side = call(
        prepare_kernel,
        [((1, rows), jnp.int32), (node_block, BF), (node_block, BF)],
        owner, nodes, source_weight, target_weight,
    )
    edge_hidden, edge_slope, message_slope, aggregate, node_hidden, node_slope, refined, sent = call(
        forward_kernel,
        [(edge_block, BF)] * 3 + [(node_block, BF)] * 4 + [((slots, 2 * width), BF)],
        *halo, own_source, target_side, nodes, cotangent, senders, receivers, slot,
        source_weight, edge_weight, inner_weight, outer_weight,
        far_in=2, far_out=3,
        scratch=[((extended + rows, width), BF), (edge_block, BF), ((rows, edges), BF)]
        + [((2 * width, width), BF), ((width, width), BF)] + [(edge_block, BF)] * 3,
        sems=[(2,), (3, edges // CHUNK)],
        where=where,
    )
    arrived = trade_slots(sent, devices)
    members, picks, counts = call(
        members_kernel,
        [((coarse_rows, slots), BF), ((slots, coarse_rows), BF), ((coarse_rows, LANES), F32)],
        table,
    )
    sent, coarse, grad_coarse = call(
        coarse_kernel,
        [((slots, 2 * width), BF)] + [((coarse_rows, width), BF)] * 2,
        arrived, members, picks, counts, coarse_weight,
    )
    returned = trade_slots(sent, devices)
    grad_aggregate, grad_hidden, keep, give = call(
        node_back_kernel,
        [(node_block, BF), (node_block, BF), ((4 * packed, LANES), BF), ((4 * packed, LANES), BF)],
        returned, slot, cotangent, nodes, aggregate, node_hidden, node_slope, coarse, grad_coarse,
        inner_weight, outer_weight,
        where=where, scale=scale,
    )
    early = paired(keep, give)
    early_rows = 4 * packed // chips
    early = total(trade_chips(early.reshape(chips, early_rows, LANES)))
    keep, give, grad_sources, grad_targets, *back = call(
        edge_back_kernel,
        [((3 * packed, LANES), BF)] * 2 + [((extended, width), BF), (node_block, BF)] + halo_blocks,
        senders, receivers, grad_aggregate, *halo, nodes, edge_weight, source_weight,
        edge_slope, message_slope, edge_hidden,
        far_in=3,
        scratch=[(edge_block, BF)] * 5 + [((extended, edges), BF), ((rows, edges), BF), ((extended, width), BF)],
        sems=[(3, edges // CHUNK)],
        where=where, scale=scale,
    )
    halo_back = trade_halo(back)
    late = paired(keep, give)
    late_rows = 3 * packed // chips
    late = total(trade_chips(late.reshape(chips, late_rows, LANES)))
    sent = jnp.concatenate([early, late], axis=0)
    sent = jnp.broadcast_to(sent[None], (chips,) + sent.shape)
    mine = trade_chips(sent)
    updated, node_gradient = call(
        finish_kernel,
        [(node_block, BF), (node_block, F32)],
        returned, slot, cotangent, refined, grad_hidden, grad_sources, grad_targets, halo_lists, *halo_back,
        inner_weight, source_weight, target_weight,
        where=where,
    )
    shapes = [square, square, square, ((2 * width, width), F32), square, square]
    buffers = {"scratch": [((7 * width // 2, width), F32)], "sems": [(7,)], "far_out": 6, "where": where}
    results = call(results_kernel, shapes, mine, **buffers, early=early_rows, other=False)
    results = call(
        results_kernel, shapes, across(mine), *results, far_in=6, aliases=6,
        **buffers, early=early_rows, other=True,
    )
    return (updated, node_gradient, *results)


def solution(mesh):
    whole = mesh.devices.reshape(mesh.shape["row"] // 2, 2, -1, 4)
    mesh = Mesh(whole, ALL)
    in_specs = (
        P(ALL, None),
        P(ALL, None),
        P(ALL),
        P(ALL),
        P(ALL, None, None),
        P(ALL),
        P(ALL, None),
        P(),
        P(),
        P(),
        P(),
        P(),
        P(),
    )
    out_specs = (P(ALL, None), P(ALL, None), P(), P(), P(), P(), P(), P())

    return jax.shard_map(local, mesh=mesh, in_specs=in_specs, out_specs=out_specs, check_vma=False)
```

```python
import functools
import math

import jax
import jax.numpy as jnp
from jax import lax
from jax.experimental import pallas as pl
from jax.experimental.pallas import tpu as pltpu
from jax.sharding import Mesh
from jax.sharding import PartitionSpec as P


BF = jnp.bfloat16
F32 = jnp.float32
LANES = 128
CHUNK = 1024
SMALL = 32
LARGE = 60
CAPACITY = 8
ROW = ("z", "core")
COL = ("x", "y")
CHIPS = ("z", "x", "y")
ALL = ROW + COL


def dot(first, second):
    return jnp.dot(first, second, preferred_element_type=F32)


def left_dot(first, second):
    return lax.dot_general(
        first, second, (((0,), (0,)), ((), ())), preferred_element_type=F32
    )


def right_dot(first, second):
    return lax.dot_general(
        first, second, (((1,), (1,)), ((), ())), preferred_element_type=F32
    )


def iota(shape, axis):
    return lax.broadcasted_iota(jnp.int32, shape, axis)


def column(row):
    square = (row.shape[1],) * 2
    eye = iota(square, 0) == iota(square, 1)
    spread = jnp.broadcast_to(row.astype(F32), square)
    return jnp.sum(jnp.where(eye, spread, 0.0), axis=1, keepdims=True).astype(jnp.int32)


def hot(mask):
    return jnp.where(mask, 1.0, 0.0).astype(BF)


def wide_column(row):
    return jnp.concatenate(
        [column(row[:, k : k + LANES]) for k in range(0, row.shape[1], LANES)], axis=0
    )


def wide_row(ref):
    return jnp.concatenate([ref[k : k + 1, :] for k in range(ref.shape[0])], axis=1)


def gates(value):
    sigma = 0.5 * jnp.tanh(0.5 * value) + 0.5
    active = value * sigma
    return active, sigma + active * (1.0 - sigma)


def sent_order(where):
    return where[0], 1 - where[0], 2 + where[1], 3 - where[1]


def received_order(where):
    return 1 - where[0], where[0], 3 - where[1], 2 + where[1]


def block(at, base, rows):
    return pl.ds(pl.multiple_of(base + at * rows, rows), rows)


def halo_picks(where, lists, rows):
    length = lists.shape[2]
    columns = [column(lists[0, pl.ds(at, 1), :]) for at in sent_order(where)]
    return jnp.concatenate([hot(each == iota((length, rows), 1)) for each in columns], axis=0)


def halo_kernel(where, nodes, lists, *outs):
    picked = dot(halo_picks(where, lists, nodes.shape[0]), nodes[...]).astype(BF)
    rows = outs[0].shape[0]
    for number, out in enumerate(outs):
        out[...] = picked[number * rows : (number + 1) * rows, :]


def prepare_kernel(owner, nodes, source_weight, target_weight, slot_out, own_source, target_side):
    rows = nodes.shape[0]
    owner_row = wide_row(owner)
    owner_column = wide_column(owner_row)
    square = (rows, rows)
    before = (owner_column == owner_row) & (iota(square, 0) < iota(square, 1))
    rank = jnp.sum(jnp.where(before, 1.0, 0.0), axis=0, keepdims=True).astype(jnp.int32)
    slot_out[...] = owner_row * CAPACITY + rank
    own_source[...] = dot(nodes[...], source_weight[...]).astype(BF)
    target_side[...] = dot(nodes[...], target_weight[...]).astype(BF)


def chunk(turn):
    return slice(turn * CHUNK, (turn + 1) * CHUNK)


def forward_kernel(
    where, halo_0, halo_1, halo_2, halo_3, own_source, target_side, nodes, cotangent, edge_source, edge_target, slot,
    source_weight, edge_weight, inner_far, outer_far,
    edge_hidden, edge_slope, message_slope, aggregate, node_hidden, node_slope, refined, sent,
    sides, active, spread, inner_weight, outer_weight, hidden_kept, slope_kept, message_kept, weight_sems, sems,
):
    fetches = [
        pltpu.make_async_copy(inner_far, inner_weight, weight_sems.at[0]),
        pltpu.make_async_copy(outer_far, outer_weight, weight_sems.at[1]),
    ]
    for fetch in fetches:
        fetch.start()
    rows, width = nodes.shape
    extended = rows + LANES
    edges = hidden_kept.shape[0]
    sides[:rows, :] = own_source[...]
    halo = jnp.concatenate([halo_0[...], halo_1[...], halo_2[...], halo_3[...]], axis=0)
    halo = dot(halo, source_weight[...]).astype(BF)
    length = halo_0.shape[0]
    for number, at in enumerate(received_order(where)):
        sides[block(at, rows, length), :] = halo[number * length : (number + 1) * length, :]
    sides[extended:, :] = target_side[...]
    group = CHUNK // LANES
    stores = []
    for turn in range(edges // CHUNK):
        span = chunk(turn)
        picks = []
        for at in range(turn * group, (turn + 1) * group):
            senders = edge_source[at : at + 1, :]
            receivers = edge_target[at : at + 1, :]
            sender_hot = hot(column(senders) == iota((LANES, extended), 1))
            receiver_hot = hot(column(receivers) == iota((LANES, rows), 1))
            picks.append(jnp.concatenate([sender_hot, receiver_hot], axis=1))
            spread[:, at * LANES : (at + 1) * LANES] = hot(iota((rows, LANES), 0) == receivers)
        hidden, slope = gates(dot(jnp.concatenate(picks, axis=0), sides[...]))
        hidden = hidden.astype(BF)
        hidden_kept[span, :] = hidden
        slope_kept[span, :] = slope.astype(BF)
        message, slope = gates(dot(hidden, edge_weight[...]))
        active[span, :] = message.astype(BF)
        message_kept[span, :] = slope.astype(BF)
        pairs = ((hidden_kept, edge_hidden), (slope_kept, edge_slope), (message_kept, message_slope))
        for number, (kept, out) in enumerate(pairs):
            stores.append(pltpu.make_async_copy(kept.at[span, :], out.at[span, :], sems.at[number, turn]))
            stores[-1].start()
    gathered = dot(spread[...], active[...]).astype(BF)
    aggregate[...] = gathered
    for fetch in fetches:
        fetch.wait()
    linear = dot(nodes[...], inner_weight[:width, :]) + dot(gathered, inner_weight[width:, :])
    hidden, slope = gates(linear)
    hidden = hidden.astype(BF)
    node_hidden[...] = hidden
    node_slope[...] = slope.astype(BF)
    result = (nodes[...].astype(F32) + dot(hidden, outer_weight[...])).astype(BF)
    refined[...] = result
    place = hot(iota((sent.shape[0], rows), 0) == slot[...])
    sent[:, :width] = dot(place, result).astype(BF)
    sent[:, width:] = dot(place, cotangent[...]).astype(BF)
    for store in stores:
        store.wait()


def coarse_kernel(arrived, table, weight, out, coarse_out, grad_out):
    rows, width = coarse_out.shape
    row = wide_row(table)
    members = jnp.where(iota((rows, row.shape[1]), 0) == row, 1.0, 0.0)
    count = jnp.maximum(jnp.sum(members, axis=1, keepdims=True), 1.0)
    picks = hot(wide_column(row) == iota((row.shape[1], rows), 1))
    totals = dot(members.astype(BF), arrived[...])
    coarse = (totals[:, :width] / count).astype(BF)
    coarse_out[...] = coarse
    active, slope = gates(dot(coarse, weight[...]))
    grad = (totals[:, width:] * slope).astype(BF)
    grad_out[...] = grad
    share = (right_dot(grad, weight[...]) / count).astype(BF)
    out[:, :width] = dot(picks, share).astype(BF)
    out[:, width:] = dot(picks, active.astype(BF)).astype(BF)


def half_of(ref, half):
    columns = ref.shape[1] // 2
    return ref[:, pl.ds(pl.multiple_of(half * columns, columns), columns)]


def pack(out, at, value):
    rows, width = value.shape
    for k in range(width // LANES):
        out[at * width // LANES + k * rows : at * width // LANES + (k + 1) * rows, :] = value[
            :, k * LANES : (k + 1) * LANES
        ].astype(BF)


def halves(scale, where, keep, give, pairs):
    at = 0
    for first, second in pairs:
        for out, half in ((keep, where[0]), (give, 1 - where[0])):
            pack(out, at, left_dot(half_of(first, half), second) * scale)
        at += first.shape[1] // 2


def node_back_kernel(
    scale, where, returned, slot, cotangent, nodes, aggregate, node_hidden, node_slope, coarse, grad_coarse,
    inner_weight, outer_weight,
    grad_aggregate, grad_hidden, keep, give,
):
    rows, width = nodes.shape
    picks = hot(wide_column(slot[...]) == iota((rows, returned.shape[0]), 1))
    grad = cotangent[...].astype(F32) + dot(picks, returned[:, :width])
    low = grad.astype(BF)
    hidden = (right_dot(low, outer_weight[...]) * node_slope[...].astype(F32)).astype(BF)
    grad_hidden[...] = hidden
    grad_aggregate[...] = right_dot(hidden, inner_weight[width:, :]).astype(BF)
    pairs = ((node_hidden, low), (nodes, hidden), (aggregate, hidden), (coarse, grad_coarse[...]))
    halves(scale, where, keep, give, pairs)


def edge_back_kernel(
    scale, where, edge_source, edge_target, grad_aggregate, halo_0, halo_1, halo_2, halo_3, nodes, edge_weight,
    source_weight, edge_slope, message_slope, edge_hidden,
    keep, give, grad_sources, grad_targets, back_0, back_1, back_2, back_3,
    slope_kept, message_kept, hidden_kept, grad_message, grad_edges, source_spread, target_spread, extended, sems,
):
    rows, _ = nodes.shape
    table = grad_sources.shape[0]
    edges = slope_kept.shape[0]
    turns = edges // CHUNK
    group = CHUNK // LANES
    fetches = []
    for turn in range(turns):
        span = chunk(turn)
        for number, (far, kept) in enumerate(((message_slope, message_kept), (edge_slope, slope_kept))):
            fetches.append(pltpu.make_async_copy(far.at[span, :], kept.at[span, :], sems.at[number, turn]))
    fetches.append(pltpu.make_async_copy(edge_hidden, hidden_kept, sems.at[2, 0]))
    for fetch in fetches:
        fetch.start()
    extended[:rows, :] = nodes[...]
    length = halo_0.shape[0]
    received = received_order(where)
    for at, halo in zip(received, (halo_0, halo_1, halo_2, halo_3)):
        extended[block(at, rows, length), :] = halo[...]
    for turn in range(turns):
        span = chunk(turn)
        picks = []
        for at in range(turn * group, (turn + 1) * group):
            senders = edge_source[at : at + 1, :]
            receivers = edge_target[at : at + 1, :]
            lanes = slice(at * LANES, (at + 1) * LANES)
            picks.append(hot(column(receivers) == iota((LANES, rows), 1)))
            source_spread[:, lanes] = hot(iota((table, LANES), 0) == senders)
            target_spread[:, lanes] = hot(iota((rows, LANES), 0) == receivers)
        taken = dot(jnp.concatenate(picks, axis=0), grad_aggregate[...])
        fetches[2 * turn].wait()
        message = (taken * message_kept[span, :].astype(F32)).astype(BF)
        grad_message[span, :] = message
        fetches[2 * turn + 1].wait()
        grad = right_dot(message, edge_weight[...]) * slope_kept[span, :].astype(F32)
        grad_edges[span, :] = grad.astype(BF)
    sources = dot(source_spread[...], grad_edges[...]).astype(BF)
    targets = dot(target_spread[...], grad_edges[...]).astype(BF)
    grad_sources[...] = sources
    grad_targets[...] = targets
    back = jnp.concatenate([grad_sources[block(at, rows, length), :] for at in received], axis=0)
    back = right_dot(back, source_weight[...]).astype(BF)
    for number, out in enumerate((back_0, back_1, back_2, back_3)):
        out[...] = back[number * length : (number + 1) * length, :]
    fetches[-1].wait()
    pairs = ((hidden_kept, grad_message[...]), (extended, sources), (nodes, targets))
    halves(scale, where, keep, give, pairs)


def finish_kernel(
    where, returned, slot, cotangent, refined, grad_hidden, grad_sources, grad_targets, lists,
    back_0, back_1, back_2, back_3, inner_weight, source_weight, target_weight,
    updated, node_gradient,
):
    rows, width = refined.shape
    picks = hot(wide_column(slot[...]) == iota((rows, returned.shape[0]), 1))
    updated[...] = (refined[...].astype(F32) + dot(picks, returned[:, width:])).astype(BF)
    back = jnp.concatenate([back_0[...], back_1[...], back_2[...], back_3[...]], axis=0)
    places = halo_picks(where, lists, rows)
    node_gradient[...] = (
        cotangent[...].astype(F32)
        + dot(picks, returned[:, :width])
        + right_dot(grad_hidden[...], inner_weight[:width, :])
        + right_dot(grad_targets[...], target_weight[...])
        + right_dot(grad_sources[:rows, :], source_weight[...])
        + left_dot(places, back)
    )


def results_kernel(early, other, where, gathered, *refs):
    outs, wide, sems = refs[-8:-2], refs[-2], refs[-1]
    source, target, edge, inner, outer, coarse = outs
    which = 1 - where[0] if other else where[0]
    width = wide.shape[1]
    half = width // 2
    blocks = width // LANES
    peers, rows, lanes = gathered.shape
    first = gathered[:, :early, :].astype(F32).reshape(peers * early, lanes)
    second = gathered[:, early:, :].astype(F32).reshape(peers * (rows - early), lanes)
    places = ((outer, 0, first, 0), (inner, 0, first, 1), (inner, width, first, 2), (coarse, 0, first, 3))
    places += ((edge, 0, second, 0), (source, 0, second, 1), (target, 0, second, 2))
    stores = []
    for number, (out, base, values, at) in enumerate(places):
        own = slice(number * half, (number + 1) * half)
        for k in range(blocks):
            start = (at * blocks + k) * half
            wide[own, k * LANES : (k + 1) * LANES] = values[start : start + half, :]
        span = pl.ds(pl.multiple_of(base + which * half, half), half)
        stores.append(pltpu.make_async_copy(wide.at[own, :], out.at[span, :], sems.at[number]))
        stores[-1].start()
    for store in stores:
        store.wait()


def call(kernel, outs, *args, far_in=0, far_out=0, scratch=(), sems=(), where=None, aliases=0, grant=LARGE, **static):
    body = functools.partial(kernel, *static.values())
    near, far = pl.BlockSpec(memory_space=pltpu.VMEM), pl.BlockSpec(memory_space=pl.ANY)
    specs = [near] * (len(args) - far_in) + [far] * far_in
    if where is not None:
        args, specs = (where,) + args, [pl.BlockSpec(memory_space=pltpu.SMEM)] + specs
    return pl.pallas_call(
        body,
        in_specs=specs,
        out_specs=[far] * far_out + [near] * (len(outs) - far_out),
        out_shape=[jax.ShapeDtypeStruct(shape, dtype) for shape, dtype in outs],
        scratch_shapes=[pltpu.VMEM(shape, dtype) for shape, dtype in scratch]
        + [pltpu.SemaphoreType.DMA(shape) for shape in sems],
        compiler_params=pltpu.CompilerParams(vmem_limit_bytes=grant * 2 ** 20),
        input_output_aliases={len(args) - aliases + k: k for k in range(aliases)},
    )(*args)


def swapped(value, axis, first):
    count = math.prod(lax.axis_size(name) for name in axis)
    lower = range(first, count - 1, 2)
    pairs = [(at, at + 1) for at in lower] + [(at + 1, at) for at in lower]
    return lax.ppermute(value, axis, pairs)


def trade_halo(blocks):
    moved = []
    for number, (axis, first) in enumerate(((ROW, 0), (ROW, 1), (COL, 0), (COL, 1))):
        moved.append(swapped(blocks[number], axis, first))
    return moved


def trade_slots(buffer, devices):
    slots, width = buffer.shape
    shaped = buffer.reshape(devices, slots // devices, width)
    moved = lax.all_to_all(shaped, ALL, split_axis=0, concat_axis=0, tiled=True)
    return moved.reshape(slots, width)


def across(value):
    return lax.ppermute(value, "core", [(0, 1), (1, 0)])


def paired(keep, give):
    return (keep.astype(F32) + across(give).astype(F32)).astype(BF)


def trade_chips(value):
    return lax.all_to_all(value, CHIPS, split_axis=0, concat_axis=0, tiled=True)


def total(arrived):
    return jnp.sum(arrived.astype(F32), axis=0).astype(BF)


def local(
    nodes,
    cotangent,
    edge_source,
    edge_target,
    halo_lists,
    pool_owner,
    pool_table,
    source_weight,
    target_weight,
    edge_weight,
    inner_weight,
    outer_weight,
    coarse_weight,
):
    chips = math.prod(lax.axis_size(name) for name in CHIPS)
    devices = 2 * chips
    where = jnp.stack([lax.axis_index("core"), lax.axis_index("y") % 2])
    rows, width = nodes.shape
    edges = edge_source.shape[0]
    halo_rows = halo_lists.shape[2]
    extended = rows + 4 * halo_rows
    slots = pool_table.shape[1]
    coarse_rows = rows // 4
    scale = 1.0 / math.sqrt(rows * devices)
    owner = pool_owner.reshape(rows // LANES, LANES)
    table = pool_table.reshape(slots // LANES, LANES)
    senders = edge_source.reshape(edges // LANES, LANES)
    receivers = edge_target.reshape(edges // LANES, LANES)
    node_block, edge_block = (rows, width), (edges, width)
    square = ((width, width), F32)
    packed = width // 2 * width // LANES

    halo_blocks = [((halo_rows, width), BF)] * 4
    halo = trade_halo(call(halo_kernel, halo_blocks, nodes, halo_lists, where=where))
    slot, own_source, target_side = call(
        prepare_kernel,
        [((1, rows), jnp.int32), (node_block, BF), (node_block, BF)],
        owner, nodes, source_weight, target_weight,
    )
    edge_hidden, edge_slope, message_slope, aggregate, node_hidden, node_slope, refined, sent = call(
        forward_kernel,
        [(edge_block, BF)] * 3 + [(node_block, BF)] * 4 + [((slots, 2 * width), BF)],
        *halo, own_source, target_side, nodes, cotangent, senders, receivers, slot,
        source_weight, edge_weight, inner_weight, outer_weight,
        far_in=2, far_out=3,
        scratch=[((extended + rows, width), BF), (edge_block, BF), ((rows, edges), BF)]
        + [((2 * width, width), BF), ((width, width), BF)] + [(edge_block, BF)] * 3,
        sems=[(2,), (3, edges // CHUNK)],
        where=where,
    )
    arrived = trade_slots(sent, devices)
    sent, coarse, grad_coarse = call(
        coarse_kernel,
        [((slots, 2 * width), BF)] + [((coarse_rows, width), BF)] * 2,
        arrived, table, coarse_weight,
        grant=SMALL,
    )
    returned = trade_slots(sent, devices)
    grad_aggregate, grad_hidden, keep, give = call(
        node_back_kernel,
        [(node_block, BF), (node_block, BF), ((4 * packed, LANES), BF), ((4 * packed, LANES), BF)],
        returned, slot, cotangent, nodes, aggregate, node_hidden, node_slope, coarse, grad_coarse,
        inner_weight, outer_weight,
        where=where, grant=SMALL, scale=scale,
    )
    early = paired(keep, give)
    early_rows = 4 * packed // chips
    early = total(trade_chips(early.reshape(chips, early_rows, LANES)))
    keep, give, grad_sources, grad_targets, *back = call(
        edge_back_kernel,
        [((3 * packed, LANES), BF)] * 2 + [((extended, width), BF), (node_block, BF)] + halo_blocks,
        senders, receivers, grad_aggregate, *halo, nodes, edge_weight, source_weight,
        edge_slope, message_slope, edge_hidden,
        far_in=3,
        scratch=[(edge_block, BF)] * 5 + [((extended, edges), BF), ((rows, edges), BF), ((extended, width), BF)],
        sems=[(3, edges // CHUNK)],
        where=where, scale=scale,
    )
    halo_back = trade_halo(back)
    late = paired(keep, give)
    late_rows = 3 * packed // chips
    late = total(trade_chips(late.reshape(chips, late_rows, LANES)))
    sent = jnp.concatenate([early, late], axis=0)
    sent = jnp.broadcast_to(sent[None], (chips,) + sent.shape)
    mine = trade_chips(sent)
    updated, node_gradient = call(
        finish_kernel,
        [(node_block, BF), (node_block, F32)],
        returned, slot, cotangent, refined, grad_hidden, grad_sources, grad_targets, halo_lists, *halo_back,
        inner_weight, source_weight, target_weight,
        where=where,
    )
    shapes = [square, square, square, ((2 * width, width), F32), square, square]
    buffers = {"scratch": [((7 * width // 2, width), F32)], "sems": [(7,)], "far_out": 6, "where": where, "grant": SMALL}
    results = call(results_kernel, shapes, mine, **buffers, early=early_rows, other=False)
    results = call(
        results_kernel, shapes, across(mine), *results, far_in=6, aliases=6,
        **buffers, early=early_rows, other=True,
    )
    return (updated, node_gradient, *results)


def solution(mesh):
    whole = mesh.devices.reshape(mesh.shape["row"] // 2, 2, -1, 4)
    mesh = Mesh(whole, ALL)
    in_specs = (
        P(ALL, None),
        P(ALL, None),
        P(ALL),
        P(ALL),
        P(ALL, None, None),
        P(ALL),
        P(ALL, None),
        P(),
        P(),
        P(),
        P(),
        P(),
        P(),
    )
    out_specs = (P(ALL, None), P(ALL, None), P(), P(), P(), P(), P(), P())

    return jax.shard_map(local, mesh=mesh, in_specs=in_specs, out_specs=out_specs, check_vma=False)
```

```python
import functools
import math

import jax
import jax.numpy as jnp
from jax import lax
from jax.experimental import pallas as pl
from jax.experimental.pallas import tpu as pltpu
from jax.sharding import Mesh
from jax.sharding import PartitionSpec as P


BF = jnp.bfloat16
F32 = jnp.float32
LANES = 128
CHUNK = 1024
BACK_CHUNK = 2048
SMALL = 32
LARGE = 60
CAPACITY = 8
ROW = ("z", "core")
COL = ("x", "y")
CHIPS = ("z", "x", "y")
ALL = ROW + COL


def dot(first, second):
    return jnp.dot(first, second, preferred_element_type=F32)


def left_dot(first, second):
    return lax.dot_general(
        first, second, (((0,), (0,)), ((), ())), preferred_element_type=F32
    )


def right_dot(first, second):
    return lax.dot_general(
        first, second, (((1,), (1,)), ((), ())), preferred_element_type=F32
    )


def iota(shape, axis):
    return lax.broadcasted_iota(jnp.int32, shape, axis)


def column(row):
    square = (row.shape[1],) * 2
    eye = iota(square, 0) == iota(square, 1)
    spread = jnp.broadcast_to(row.astype(F32), square)
    return jnp.sum(jnp.where(eye, spread, 0.0), axis=1, keepdims=True).astype(jnp.int32)


def hot(mask):
    return jnp.where(mask, 1.0, 0.0).astype(BF)


def wide_column(row):
    return jnp.concatenate(
        [column(row[:, k : k + LANES]) for k in range(0, row.shape[1], LANES)], axis=0
    )


def wide_row(ref):
    return jnp.concatenate([ref[k : k + 1, :] for k in range(ref.shape[0])], axis=1)


def gates(value):
    sigma = 0.5 * jnp.tanh(0.5 * value) + 0.5
    active = value * sigma
    return active, sigma + active * (1.0 - sigma)


def sent_order(where):
    return where[0], 1 - where[0], 2 + where[1], 3 - where[1]


def received_order(where):
    return 1 - where[0], where[0], 3 - where[1], 2 + where[1]


def block(at, base, rows):
    return pl.ds(pl.multiple_of(base + at * rows, rows), rows)


def halo_picks(where, lists, rows):
    length = lists.shape[2]
    columns = [column(lists[0, pl.ds(at, 1), :]) for at in sent_order(where)]
    return jnp.concatenate([hot(each == iota((length, rows), 1)) for each in columns], axis=0)


def halo_kernel(where, nodes, lists, *outs):
    picked = dot(halo_picks(where, lists, nodes.shape[0]), nodes[...]).astype(BF)
    rows = outs[0].shape[0]
    for number, out in enumerate(outs):
        out[...] = picked[number * rows : (number + 1) * rows, :]


def prepare_kernel(owner, nodes, source_weight, target_weight, slot_out, own_source, target_side):
    rows = nodes.shape[0]
    owner_row = wide_row(owner)
    owner_column = wide_column(owner_row)
    square = (rows, rows)
    before = (owner_column == owner_row) & (iota(square, 0) < iota(square, 1))
    rank = jnp.sum(jnp.where(before, 1.0, 0.0), axis=0, keepdims=True).astype(jnp.int32)
    slot_out[...] = owner_row * CAPACITY + rank
    own_source[...] = dot(nodes[...], source_weight[...]).astype(BF)
    target_side[...] = dot(nodes[...], target_weight[...]).astype(BF)


def chunk(turn, length):
    return slice(turn * length, (turn + 1) * length)


def forward_kernel(
    where, halo_0, halo_1, halo_2, halo_3, own_source, target_side, nodes, cotangent, edge_source, edge_target, slot,
    source_weight, edge_weight, inner_far, outer_far,
    edge_hidden, edge_slope, message_slope, aggregate, node_hidden, node_slope, refined, sent,
    sides, active, spread, inner_weight, outer_weight, hidden_kept, slope_kept, message_kept,
    aggregate_kept, node_kept, weight_sems, sems, node_sems,
):
    fetches = [
        pltpu.make_async_copy(inner_far, inner_weight, weight_sems.at[0]),
        pltpu.make_async_copy(outer_far, outer_weight, weight_sems.at[1]),
    ]
    for fetch in fetches:
        fetch.start()
    rows, width = nodes.shape
    extended = rows + LANES
    edges = hidden_kept.shape[0]
    sides[:rows, :] = own_source[...]
    halo = jnp.concatenate([halo_0[...], halo_1[...], halo_2[...], halo_3[...]], axis=0)
    halo = dot(halo, source_weight[...]).astype(BF)
    length = halo_0.shape[0]
    for number, at in enumerate(received_order(where)):
        sides[block(at, rows, length), :] = halo[number * length : (number + 1) * length, :]
    sides[extended:, :] = target_side[...]
    group = CHUNK // LANES
    stores = []
    for turn in range(edges // CHUNK):
        span = chunk(turn, CHUNK)
        picks = []
        for at in range(turn * group, (turn + 1) * group):
            senders = edge_source[at : at + 1, :]
            receivers = edge_target[at : at + 1, :]
            sender_hot = hot(column(senders) == iota((LANES, extended), 1))
            receiver_hot = hot(column(receivers) == iota((LANES, rows), 1))
            picks.append(jnp.concatenate([sender_hot, receiver_hot], axis=1))
            spread[:, at * LANES : (at + 1) * LANES] = hot(iota((rows, LANES), 0) == receivers)
        hidden, slope = gates(dot(jnp.concatenate(picks, axis=0), sides[...]))
        hidden = hidden.astype(BF)
        hidden_kept[span, :] = hidden
        slope_kept[span, :] = slope.astype(BF)
        message, slope = gates(dot(hidden, edge_weight[...]))
        active[span, :] = message.astype(BF)
        message_kept[span, :] = slope.astype(BF)
        pairs = ((hidden_kept, edge_hidden), (slope_kept, edge_slope), (message_kept, message_slope))
        for number, (kept, out) in enumerate(pairs):
            stores.append(pltpu.make_async_copy(kept.at[span, :], out.at[span, :], sems.at[number, turn]))
            stores[-1].start()
    gathered = dot(spread[...], active[...]).astype(BF)
    aggregate_kept[...] = gathered
    stores.append(pltpu.make_async_copy(aggregate_kept, aggregate, node_sems.at[0]))
    stores[-1].start()
    for fetch in fetches:
        fetch.wait()
    linear = dot(nodes[...], inner_weight[:width, :]) + dot(gathered, inner_weight[width:, :])
    hidden, slope = gates(linear)
    hidden = hidden.astype(BF)
    node_kept[0] = hidden
    node_kept[1] = slope.astype(BF)
    for number, out in enumerate((node_hidden, node_slope)):
        stores.append(pltpu.make_async_copy(node_kept.at[number], out, node_sems.at[1 + number]))
        stores[-1].start()
    result = (nodes[...].astype(F32) + dot(hidden, outer_weight[...])).astype(BF)
    refined[...] = result
    place = hot(iota((sent.shape[0], rows), 0) == slot[...])
    sent[:, :width] = dot(place, result).astype(BF)
    sent[:, width:] = dot(place, cotangent[...]).astype(BF)
    for store in stores:
        store.wait()


def coarse_kernel(arrived, table, weight, out, coarse_out, grad_out):
    rows, width = coarse_out.shape
    row = wide_row(table)
    members = jnp.where(iota((rows, row.shape[1]), 0) == row, 1.0, 0.0)
    count = jnp.maximum(jnp.sum(members, axis=1, keepdims=True), 1.0)
    picks = hot(wide_column(row) == iota((row.shape[1], rows), 1))
    totals = dot(members.astype(BF), arrived[...])
    coarse = (totals[:, :width] / count).astype(BF)
    coarse_out[...] = coarse
    active, slope = gates(dot(coarse, weight[...]))
    grad = (totals[:, width:] * slope).astype(BF)
    grad_out[...] = grad
    share = (right_dot(grad, weight[...]) / count).astype(BF)
    out[:, :width] = dot(picks, share).astype(BF)
    out[:, width:] = dot(picks, active.astype(BF)).astype(BF)


def half_of(ref, half):
    columns = ref.shape[1] // 2
    return ref[:, pl.ds(pl.multiple_of(half * columns, columns), columns)]


def pack(out, at, value):
    rows, width = value.shape
    for k in range(width // LANES):
        out[at * width // LANES + k * rows : at * width // LANES + (k + 1) * rows, :] = value[
            :, k * LANES : (k + 1) * LANES
        ].astype(BF)


def halves(scale, where, keep, give, pairs):
    at = 0
    for first, second in pairs:
        for out, half in ((keep, where[0]), (give, 1 - where[0])):
            pack(out, at, left_dot(half_of(first, half), second) * scale)
        at += first.shape[1] // 2


def node_back_kernel(
    scale, where, returned, slot, cotangent, nodes, aggregate, node_hidden, node_slope, coarse, grad_coarse,
    inner_weight, outer_weight,
    grad_aggregate, grad_hidden, keep, give,
):
    rows, width = nodes.shape
    picks = hot(wide_column(slot[...]) == iota((rows, returned.shape[0]), 1))
    grad = cotangent[...].astype(F32) + dot(picks, returned[:, :width])
    low = grad.astype(BF)
    hidden = (right_dot(low, outer_weight[...]) * node_slope[...].astype(F32)).astype(BF)
    grad_hidden[...] = hidden
    grad_aggregate[...] = right_dot(hidden, inner_weight[width:, :]).astype(BF)
    pairs = ((node_hidden, low), (nodes, hidden), (aggregate, hidden), (coarse, grad_coarse[...]))
    halves(scale, where, keep, give, pairs)


def edge_back_kernel(
    scale, where, edge_source, edge_target, grad_aggregate, halo_0, halo_1, halo_2, halo_3, nodes, edge_weight,
    source_weight, edge_slope, message_slope, edge_hidden,
    keep, give, grad_sources, grad_targets, back_0, back_1, back_2, back_3,
    slope_kept, message_kept, hidden_kept, grad_message, grad_edges, source_spread, target_spread, extended, sems,
):
    rows, _ = nodes.shape
    table = grad_sources.shape[0]
    edges = slope_kept.shape[0]
    turns = edges // BACK_CHUNK
    group = BACK_CHUNK // LANES
    fetches = []
    for turn in range(turns):
        span = chunk(turn, BACK_CHUNK)
        for number, (far, kept) in enumerate(((message_slope, message_kept), (edge_slope, slope_kept))):
            fetches.append(pltpu.make_async_copy(far.at[span, :], kept.at[span, :], sems.at[number, turn]))
    fetches.append(pltpu.make_async_copy(edge_hidden, hidden_kept, sems.at[2, 0]))
    for fetch in fetches:
        fetch.start()
    extended[:rows, :] = nodes[...]
    length = halo_0.shape[0]
    received = received_order(where)
    for at, halo in zip(received, (halo_0, halo_1, halo_2, halo_3)):
        extended[block(at, rows, length), :] = halo[...]
    for turn in range(turns):
        span = chunk(turn, BACK_CHUNK)
        picks = []
        for at in range(turn * group, (turn + 1) * group):
            senders = edge_source[at : at + 1, :]
            receivers = edge_target[at : at + 1, :]
            lanes = slice(at * LANES, (at + 1) * LANES)
            picks.append(hot(column(receivers) == iota((LANES, rows), 1)))
            source_spread[:, lanes] = hot(iota((table, LANES), 0) == senders)
            target_spread[:, lanes] = hot(iota((rows, LANES), 0) == receivers)
        taken = dot(jnp.concatenate(picks, axis=0), grad_aggregate[...])
        fetches[2 * turn].wait()
        message = (taken * message_kept[span, :].astype(F32)).astype(BF)
        grad_message[span, :] = message
        fetches[2 * turn + 1].wait()
        grad = right_dot(message, edge_weight[...]) * slope_kept[span, :].astype(F32)
        grad_edges[span, :] = grad.astype(BF)
    sources = dot(source_spread[...], grad_edges[...]).astype(BF)
    targets = dot(target_spread[...], grad_edges[...]).astype(BF)
    grad_sources[...] = sources
    grad_targets[...] = targets
    back = jnp.concatenate([grad_sources[block(at, rows, length), :] for at in received], axis=0)
    back = right_dot(back, source_weight[...]).astype(BF)
    for number, out in enumerate((back_0, back_1, back_2, back_3)):
        out[...] = back[number * length : (number + 1) * length, :]
    fetches[-1].wait()
    pairs = ((hidden_kept, grad_message[...]), (extended, sources), (nodes, targets))
    halves(scale, where, keep, give, pairs)


def finish_kernel(
    where, returned, slot, cotangent, refined, grad_hidden, grad_sources, grad_targets, lists,
    back_0, back_1, back_2, back_3, inner_weight, source_weight, target_weight,
    updated, node_gradient,
):
    rows, width = refined.shape
    picks = hot(wide_column(slot[...]) == iota((rows, returned.shape[0]), 1))
    updated[...] = (refined[...].astype(F32) + dot(picks, returned[:, width:])).astype(BF)
    back = jnp.concatenate([back_0[...], back_1[...], back_2[...], back_3[...]], axis=0)
    places = halo_picks(where, lists, rows)
    node_gradient[...] = (
        cotangent[...].astype(F32)
        + dot(picks, returned[:, :width])
        + right_dot(grad_hidden[...], inner_weight[:width, :])
        + right_dot(grad_targets[...], target_weight[...])
        + right_dot(grad_sources[:rows, :], source_weight[...])
        + left_dot(places, back)
    )


def results_kernel(early, other, where, gathered, *refs):
    outs, wide, sems = refs[-8:-2], refs[-2], refs[-1]
    source, target, edge, inner, outer, coarse = outs
    which = 1 - where[0] if other else where[0]
    width = wide.shape[1]
    half = width // 2
    blocks = width // LANES
    peers, rows, lanes = gathered.shape
    first = gathered[:, :early, :].astype(F32).reshape(peers * early, lanes)
    second = gathered[:, early:, :].astype(F32).reshape(peers * (rows - early), lanes)
    places = ((outer, 0, first, 0), (inner, 0, first, 1), (inner, width, first, 2), (coarse, 0, first, 3))
    places += ((edge, 0, second, 0), (source, 0, second, 1), (target, 0, second, 2))
    stores = []
    for number, (out, base, values, at) in enumerate(places):
        own = slice(number * half, (number + 1) * half)
        for k in range(blocks):
            start = (at * blocks + k) * half
            wide[own, k * LANES : (k + 1) * LANES] = values[start : start + half, :]
        span = pl.ds(pl.multiple_of(base + which * half, half), half)
        stores.append(pltpu.make_async_copy(wide.at[own, :], out.at[span, :], sems.at[number]))
        stores[-1].start()
    for store in stores:
        store.wait()


def call(kernel, outs, *args, far_in=0, far_out=0, scratch=(), sems=(), where=None, aliases=0, grant=LARGE, **static):
    body = functools.partial(kernel, *static.values())
    near, far = pl.BlockSpec(memory_space=pltpu.VMEM), pl.BlockSpec(memory_space=pl.ANY)
    specs = [near] * (len(args) - far_in) + [far] * far_in
    if where is not None:
        args, specs = (where,) + args, [pl.BlockSpec(memory_space=pltpu.SMEM)] + specs
    return pl.pallas_call(
        body,
        in_specs=specs,
        out_specs=[far] * far_out + [near] * (len(outs) - far_out),
        out_shape=[jax.ShapeDtypeStruct(shape, dtype) for shape, dtype in outs],
        scratch_shapes=[pltpu.VMEM(shape, dtype) for shape, dtype in scratch]
        + [pltpu.SemaphoreType.DMA(shape) for shape in sems],
        compiler_params=pltpu.CompilerParams(vmem_limit_bytes=grant * 2 ** 20),
        input_output_aliases={len(args) - aliases + k: k for k in range(aliases)},
    )(*args)


def swapped(value, axis, first):
    count = math.prod(lax.axis_size(name) for name in axis)
    lower = range(first, count - 1, 2)
    pairs = [(at, at + 1) for at in lower] + [(at + 1, at) for at in lower]
    return lax.ppermute(value, axis, pairs)


def trade_halo(blocks):
    moved = []
    for number, (axis, first) in enumerate(((ROW, 0), (ROW, 1), (COL, 0), (COL, 1))):
        moved.append(swapped(blocks[number], axis, first))
    return moved


def trade_slots(buffer, devices):
    slots, width = buffer.shape
    shaped = buffer.reshape(devices, slots // devices, width)
    moved = lax.all_to_all(shaped, ALL, split_axis=0, concat_axis=0, tiled=True)
    return moved.reshape(slots, width)


def across(value):
    return lax.ppermute(value, "core", [(0, 1), (1, 0)])


def paired(keep, give):
    return (keep.astype(F32) + across(give).astype(F32)).astype(BF)


def trade_chips(value):
    return lax.all_to_all(value, CHIPS, split_axis=0, concat_axis=0, tiled=True)


def total(arrived):
    return jnp.sum(arrived.astype(F32), axis=0).astype(BF)


def local(
    nodes,
    cotangent,
    edge_source,
    edge_target,
    halo_lists,
    pool_owner,
    pool_table,
    source_weight,
    target_weight,
    edge_weight,
    inner_weight,
    outer_weight,
    coarse_weight,
):
    chips = math.prod(lax.axis_size(name) for name in CHIPS)
    devices = 2 * chips
    where = jnp.stack([lax.axis_index("core"), lax.axis_index("y") % 2])
    rows, width = nodes.shape
    edges = edge_source.shape[0]
    halo_rows = halo_lists.shape[2]
    extended = rows + 4 * halo_rows
    slots = pool_table.shape[1]
    coarse_rows = rows // 4
    scale = 1.0 / math.sqrt(rows * devices)
    owner = pool_owner.reshape(rows // LANES, LANES)
    table = pool_table.reshape(slots // LANES, LANES)
    senders = edge_source.reshape(edges // LANES, LANES)
    receivers = edge_target.reshape(edges // LANES, LANES)
    node_block, edge_block = (rows, width), (edges, width)
    square = ((width, width), F32)
    packed = width // 2 * width // LANES

    halo_blocks = [((halo_rows, width), BF)] * 4
    halo = trade_halo(call(halo_kernel, halo_blocks, nodes, halo_lists, where=where))
    slot, own_source, target_side = call(
        prepare_kernel,
        [((1, rows), jnp.int32), (node_block, BF), (node_block, BF)],
        owner, nodes, source_weight, target_weight,
    )
    edge_hidden, edge_slope, message_slope, aggregate, node_hidden, node_slope, refined, sent = call(
        forward_kernel,
        [(edge_block, BF)] * 3 + [(node_block, BF)] * 4 + [((slots, 2 * width), BF)],
        *halo, own_source, target_side, nodes, cotangent, senders, receivers, slot,
        source_weight, edge_weight, inner_weight, outer_weight,
        far_in=2, far_out=6,
        scratch=[((extended + rows, width), BF), (edge_block, BF), ((rows, edges), BF)]
        + [((2 * width, width), BF), ((width, width), BF)] + [(edge_block, BF)] * 3
        + [(node_block, BF), ((2, rows, width), BF)],
        sems=[(2,), (3, edges // CHUNK), (3,)],
        where=where,
    )
    arrived = trade_slots(sent, devices)
    sent, coarse, grad_coarse = call(
        coarse_kernel,
        [((slots, 2 * width), BF)] + [((coarse_rows, width), BF)] * 2,
        arrived, table, coarse_weight,
        grant=SMALL,
    )
    returned = trade_slots(sent, devices)
    grad_aggregate, grad_hidden, keep, give = call(
        node_back_kernel,
        [(node_block, BF), (node_block, BF), ((4 * packed, LANES), BF), ((4 * packed, LANES), BF)],
        returned, slot, cotangent, nodes, aggregate, node_hidden, node_slope, coarse, grad_coarse,
        inner_weight, outer_weight,
        where=where, grant=SMALL, scale=scale,
    )
    early = paired(keep, give)
    early_rows = 4 * packed // chips
    early = total(trade_chips(early.reshape(chips, early_rows, LANES)))
    keep, give, grad_sources, grad_targets, *back = call(
        edge_back_kernel,
        [((3 * packed, LANES), BF)] * 2 + [((extended, width), BF), (node_block, BF)] + halo_blocks,
        senders, receivers, grad_aggregate, *halo, nodes, edge_weight, source_weight,
        edge_slope, message_slope, edge_hidden,
        far_in=3,
        scratch=[(edge_block, BF)] * 5 + [((extended, edges), BF), ((rows, edges), BF), ((extended, width), BF)],
        sems=[(3, edges // BACK_CHUNK)],
        where=where, scale=scale,
    )
    halo_back = trade_halo(back)
    late = paired(keep, give)
    late_rows = 3 * packed // chips
    late = total(trade_chips(late.reshape(chips, late_rows, LANES)))
    sent = jnp.concatenate([early, late], axis=0)
    sent = jnp.broadcast_to(sent[None], (chips,) + sent.shape)
    mine = trade_chips(sent)
    updated, node_gradient = call(
        finish_kernel,
        [(node_block, BF), (node_block, F32)],
        returned, slot, cotangent, refined, grad_hidden, grad_sources, grad_targets, halo_lists, *halo_back,
        inner_weight, source_weight, target_weight,
        where=where,
    )
    shapes = [square, square, square, ((2 * width, width), F32), square, square]
    buffers = {"scratch": [((7 * width // 2, width), F32)], "sems": [(7,)], "far_out": 6, "where": where, "grant": SMALL}
    results = call(results_kernel, shapes, mine, **buffers, early=early_rows, other=False)
    results = call(
        results_kernel, shapes, across(mine), *results, far_in=6, aliases=6,
        **buffers, early=early_rows, other=True,
    )
    return (updated, node_gradient, *results)


def solution(mesh):
    whole = mesh.devices.reshape(mesh.shape["row"] // 2, 2, -1, 4)
    mesh = Mesh(whole, ALL)
    in_specs = (
        P(ALL, None),
        P(ALL, None),
        P(ALL),
        P(ALL),
        P(ALL, None, None),
        P(ALL),
        P(ALL, None),
        P(),
        P(),
        P(),
        P(),
        P(),
        P(),
    )
    out_specs = (P(ALL, None), P(ALL, None), P(), P(), P(), P(), P(), P())

    return jax.shard_map(local, mesh=mesh, in_specs=in_specs, out_specs=out_specs, check_vma=False)
```
